32 devices in a mesh: dp: 8 (over y, x, core), tensor: 4 (over z).
Axes of the slice: x: 2, y: 2, z: 4, core: 2. Of those that a mesh axis runs over, the one named last changes fastest.
Arguments:
- layer_input: float32 [2048, 768], P(('dp', 'tensor')), may hold values from -6 to 6
- segments: int32 [8, 256], P('dp'), may hold values from 0 to 2, as said below
- routes: int32 [2048, 2], P('dp'), may hold values from 0 to 15, all different within a row; in each aligned block of 256 rows (0 to 255, 256 to 511, ...) at most 48 rows name the same one
- gate_weights: float32 [2048, 2], P('dp'), may hold values from 0.2 to 1
- first_gain: bfloat16 [768], P(('dp', 'tensor')), may hold values from 0.5 to 1.5
- first_query: bfloat16 [768, 768], P('dp', 'tensor'), may hold values from -0.21875 to 0.21875
- first_key: bfloat16 [768, 768], P('dp', 'tensor'), may hold values from -0.21875 to 0.21875
- first_value: bfloat16 [768, 768], P('dp', 'tensor'), may hold values from -0.21875 to 0.21875
- first_output: bfloat16 [768, 768], P('tensor', 'dp'), may hold values from -0.875 to 0.875
- first_bias: bfloat16 [32, 12], P('dp', 'tensor'), may hold values from -2 to 300
- first_dense_gain: bfloat16 [768], P(('dp', 'tensor')), may hold values from 0.5 to 1.5
- first_dense_up: bfloat16 [768, 3072], P('dp', 'tensor'), may hold values from -0.21875 to 0.21875
- first_dense_down: bfloat16 [3072, 768], P('tensor', 'dp'), may hold values from -0.109375 to 0.109375
- second_gain: bfloat16 [768], P(('dp', 'tensor')), may hold values from 0.5 to 1.5
- second_query: bfloat16 [768, 768], P('dp', 'tensor'), may hold values from -0.21875 to 0.21875
- second_key: bfloat16 [768, 768], P('dp', 'tensor'), may hold values from -0.21875 to 0.21875
- second_value: bfloat16 [768, 768], P('dp', 'tensor'), may hold values from -0.21875 to 0.21875
- second_output: bfloat16 [768, 768], P('tensor', 'dp'), may hold values from -0.875 to 0.875
- second_bias: bfloat16 [32, 12], P('dp', 'tensor'), may hold values from -2 to 300
- second_expert_gain: bfloat16 [768], P(('dp', 'tensor')), may hold values from 0.5 to 1.5
- expert_up: bfloat16 [16, 768, 3072], P('dp', None, 'tensor'), may hold values from -0.21875 to 0.21875
- expert_down: bfloat16 [16, 3072, 768], P('dp', 'tensor'), may hold values from -0.109375 to 0.109375
- output_grad: float32 [2048, 768], P(('dp', 'tensor')), may hold values from -6 to 6
Outputs:
- layer_output: float32 [2048, 768], P(('dp', 'tensor'))
- input_grad: float32 [2048, 768], P(('dp', 'tensor'))
- first_gain_grad: float32 [768], P(('dp', 'tensor'))
- first_query_grad: float32 [768, 768], P('dp', 'tensor')
- first_key_grad: float32 [768, 768], P('dp', 'tensor')
- first_value_grad: float32 [768, 768], P('dp', 'tensor')
- first_output_grad: float32 [768, 768], P('tensor', 'dp')
- first_bias_grad: float32 [32, 12], P('dp', 'tensor')
- first_dense_gain_grad: float32 [768], P(('dp', 'tensor'))
- first_dense_up_grad: float32 [768, 3072], P('dp', 'tensor')
- first_dense_down_grad: float32 [3072, 768], P('tensor', 'dp')
- second_gain_grad: float32 [768], P(('dp', 'tensor'))
- second_query_grad: float32 [768, 768], P('dp', 'tensor')
- second_key_grad: float32 [768, 768], P('dp', 'tensor')
- second_value_grad: float32 [768, 768], P('dp', 'tensor')
- second_output_grad: float32 [768, 768], P('tensor', 'dp')
- second_bias_grad: float32 [32, 12], P('dp', 'tensor')
- second_expert_gain_grad: float32 [768], P(('dp', 'tensor'))
- expert_up_grad: float32 [16, 768, 3072], P('dp', None, 'tensor')
- expert_down_grad: float32 [16, 3072, 768], P('dp', 'tensor')
The draws below stay inside these ranges and needn't reach their ends.
Inputs may be any that keep to these rules, and one draw needn't show every extreme that they name: `segments`: documents of at most 2000 tokens, and at least 200 except where cut, are laid end to end over all sequences in order, so a sequence's first and last documents may be cut short. Within a sequence segment numbers start at 0 and never fall. `routes`: each token names 2 different experts. Within one sequence's 256 tokens no expert is named more than 48 times, a bound that some block reaches.
All inputs are finite; a program needn't handle non-finite values.
Results may differ from the reference program's by a relative error of at most 0.024.
Values may be sent and summed in bfloat16 or wider, within the bound.
A program may use at most 128 MiB of HBM per device.

```python
import math
import jax
import jax.numpy as jnp
import numpy as np
from jax import lax

D = 768
H = 12
DH = 64
FF = 3072
TOP = 2
BUCKETS = 32
DOC_MIN = 200
DOC_MAX = 2000
SEQ = 256
EXPERTS = 16
SEQS = 8
TOKENS = 2048
CAP = 48


def spiked_table(key):
    base_key = jax.random.fold_in(key, 1)
    bias_table = jax.random.uniform(base_key, (BUCKETS, H), jnp.float32, -2.0, 2.0)
    return bias_table


def draw_first_bias(key, part):
    return spiked_table(jax.random.fold_in(key, 11)).astype(jnp.bfloat16)


def draw_second_bias(key, part):
    return spiked_table(jax.random.fold_in(key, 12)).astype(jnp.bfloat16)


def draw_segments(key, part):
    doc_count = TOKENS // DOC_MIN + 2
    short_docs = (SEQ - 2) // DOC_MIN
    doc_lengths = jax.random.randint(jax.random.fold_in(key, 21), (doc_count,), DOC_MIN, DOC_MAX + 1, jnp.int32)
    doc_numbers = jnp.arange(doc_count, dtype=jnp.int32)
    exact_docs = (doc_numbers >= 1) & (doc_numbers <= short_docs)
    doc_lengths = jnp.where(exact_docs, jnp.int32(DOC_MIN), doc_lengths)
    start_shift = doc_lengths[0] - 1
    doc_ends = jnp.cumsum(doc_lengths) - start_shift
    positions = jnp.arange(TOKENS, dtype=jnp.int32)
    doc_of = jnp.sum((doc_ends[None, :] <= positions[:, None]).astype(jnp.int32), axis=1)
    per_sequence = doc_of.reshape(SEQS, SEQ)
    return per_sequence - per_sequence[:, :1]


def shard_levels(stream_key, extent, split, least, top_value):
    loudness, own = 1.0, jax.random.fold_in(stream_key, 6)
    for position, parts in split:
        steps = jnp.exp(jax.random.uniform(jax.random.fold_in(own, position), (parts,), jnp.float32, least / len(split), top_value / len(split)))
        loudness = loudness * jnp.repeat(steps, extent[position] // parts).reshape([-1 if axis == position else 1 for axis in range(len(extent))])
    return loudness


def routed_block(rng, own, number, rows, count, top, limit, slope):
    order = jax.random.permutation(rng, count)
    crowded, usual = load_shares(count, rows * top, limit, slope, True), load_shares(count, rows * top, limit, slope, False)
    places = jnp.arange(count)

    def named(sizes, offset_by):
        used = int((sizes > 0).sum())
        fixed = max(1, used // 4)
        moved = fixed + (places - fixed + offset_by * (used - fixed)) % max(1, count - fixed)
        return jnp.zeros((count,), jnp.int32).at[order[jnp.where(places < fixed, places, moved)]].set(jnp.asarray(sizes, jnp.int32))

    sizes = jnp.where(number % 4 == 0, named(crowded, number // 4), named(usual, number - number // 4 - 1))
    mixed = jax.random.permutation(jax.random.fold_in(own, 3), count)
    source_of, sink = mixed[0:count // 2 * 2:2], mixed[1:count // 2 * 2:2]
    margin = jnp.minimum(sizes[source_of] - 1, limit - sizes[sink]) // 2
    margin = jnp.where((source_of == order[0]) | (sink == order[0]) | (sizes[sink] == 0), 0, jnp.maximum(margin, 0))
    moved = jax.random.randint(jax.random.fold_in(own, 4), (count // 2,), 0, 1 << 20) % (margin + 1)
    sizes = sizes.at[source_of].add(-moved).at[sink].add(moved)
    members = jnp.searchsorted(jnp.cumsum(sizes), jnp.arange(rows * top), side="right").astype(jnp.int32)
    table = members.reshape(top, rows).T
    table = table[jax.random.permutation(jax.random.fold_in(own, 1), rows)]
    offset_by = jax.random.randint(jax.random.fold_in(own, 2), (rows, 1), 0, top)
    return jnp.take_along_axis(table, (jnp.arange(top)[None, :] + offset_by) % top, axis=1)


def load_shares(number_of, total, limit, skew, full):
    weights = [(1 << 20) // math.isqrt(standing ** skew) + 1 for standing in range(1, number_of + 1)]
    largest = limit if full else min(limit, max(-(-total // number_of), total * weights[0] // sum(weights)))
    least = 1 if total - largest >= number_of - 1 else 0
    counts, spare = [largest] + [least] * (number_of - 1), total - largest - least * (number_of - 1)
    while spare > 0:
        movable = [i for i in range(1, number_of) if counts[i] < largest] or [i for i in range(1, number_of) if counts[i] < limit]
        pool, left = sum([weights[i] for i in movable]), spare
        for i in movable:
            more = min(limit - counts[i], max(1, left * weights[i] // pool), spare)
            counts[i] = counts[i] + more
            spare = spare - more
    return np.array(counts)


def gaussian(stream_key, extent, width, bound, pieces=(), kind=jnp.bfloat16):
    factor_of = shard_levels(stream_key, extent, pieces, -0.22, 0.18) if pieces else 1.0
    values = jax.random.normal(stream_key, extent, jnp.float32) * width * factor_of
    return jnp.minimum(jnp.maximum(values, -bound), bound).astype(kind)


def setup_inputs(seed: int = 0) -> dict:
    splits = jax.random.split(jax.random.key(seed), 24)
    layer_input = gaussian(splits[0], (TOKENS, D), 1.0, 6.0, ((0, 32),), jnp.float32)
    segments = draw_segments(jax.random.fold_in(splits[23], 71), 0)
    routes_keys = jax.random.split(jax.random.fold_in(splits[2], 1), TOKENS // SEQ)
    routes_turns = jax.random.permutation(jax.random.fold_in(splits[2], 3), TOKENS // SEQ)
    routes = jax.vmap(lambda own, number: routed_block(jax.random.fold_in(splits[2], 2), own, number, SEQ, EXPERTS, TOP, CAP, 2))(routes_keys, routes_turns).reshape((TOKENS, TOP))
    gate_weights = jnp.clip(0.2 + 0.8 * jax.random.uniform(splits[3], (TOKENS, TOP), jnp.float32) ** shard_levels(splits[3], (TOKENS, TOP), ((0, 8),), -0.2, 0.2), 0.2, 1.0)
    first_gain = jnp.clip(1.0 + 0.1 * jax.random.normal(splits[4], (D,), jnp.float32), 0.5, 1.5).astype(jnp.bfloat16)
    first_query = gaussian(splits[5], (D, H * DH), D ** -0.5, 0.21875, ((0, 8), (1, 4)))
    first_key = gaussian(splits[6], (D, H * DH), D ** -0.5, 0.21875, ((0, 8), (1, 4)))
    first_value = gaussian(splits[7], (D, H * DH), D ** -0.5, 0.21875, ((0, 8), (1, 4)))
    first_output = gaussian(splits[8], (H * DH, D), (H * DH * 16 // SEQ) ** -0.5, 0.875, ((0, 4), (1, 8)))
    first_bias = draw_first_bias(jax.random.fold_in(splits[23], 71), 0)
    first_dense_gain = jnp.clip(1.0 + 0.1 * jax.random.normal(splits[10], (D,), jnp.float32), 0.5, 1.5).astype(jnp.bfloat16)
    first_dense_up = gaussian(splits[11], (D, FF), D ** -0.5, 0.21875, ((0, 8), (1, 4)))
    first_dense_down = gaussian(splits[12], (FF, D), FF ** -0.5, 0.109375, ((0, 4), (1, 8)))
    second_gain = jnp.clip(1.0 + 0.1 * jax.random.normal(splits[13], (D,), jnp.float32), 0.5, 1.5).astype(jnp.bfloat16)
    second_query = gaussian(splits[14], (D, H * DH), D ** -0.5, 0.21875, ((0, 8), (1, 4)))
    second_key = gaussian(splits[15], (D, H * DH), D ** -0.5, 0.21875, ((0, 8), (1, 4)))
    second_value = gaussian(splits[16], (D, H * DH), D ** -0.5, 0.21875, ((0, 8), (1, 4)))
    second_output = gaussian(splits[17], (H * DH, D), (H * DH * 16 // SEQ) ** -0.5, 0.875, ((0, 4), (1, 8)))
    second_bias = draw_second_bias(jax.random.fold_in(splits[23], 71), 0)
    second_expert_gain = jnp.clip(1.0 + 0.1 * jax.random.normal(splits[19], (D,), jnp.float32), 0.5, 1.5).astype(jnp.bfloat16)
    expert_up = gaussian(splits[20], (EXPERTS, D, FF), D ** -0.5, 0.21875, ((0, 8), (2, 4)))
    expert_down = gaussian(splits[21], (EXPERTS, FF, D), FF ** -0.5, 0.109375, ((0, 8), (1, 4)))
    output_grad = gaussian(splits[22], (TOKENS, D), 1.0, 6.0, ((0, 32),), jnp.float32)
    return dict(layer_input=layer_input, segments=segments, routes=routes, gate_weights=gate_weights, first_gain=first_gain, first_query=first_query, first_key=first_key, first_value=first_value, first_output=first_output, first_bias=first_bias, first_dense_gain=first_dense_gain, first_dense_up=first_dense_up, first_dense_down=first_dense_down, second_gain=second_gain, second_query=second_query, second_key=second_key, second_value=second_value, second_output=second_output, second_bias=second_bias, second_expert_gain=second_expert_gain, expert_up=expert_up, expert_down=expert_down, output_grad=output_grad)


EPSILON = 1e-06
NEG_FILL = -1e+30
HALF_ROOT = 0.7071067811865476
BELL_SCALE = 0.3989422804014327

def bucket_index(length, buckets):
    exact_count = buckets // 2
    distance = np.arange(length)
    result = np.minimum(distance, exact_count)
    for bucket_level in range(1, exact_count):
        threshold = int(np.ceil(exact_count * (128.0 / exact_count) ** (bucket_level / exact_count)))
        result = result + (distance >= threshold)
    return result.astype(np.int32)

def round_trip(values):
    return lax.optimization_barrier(values.astype(jnp.bfloat16)).astype(jnp.float32)

def gelu_value(inputs):
    return 0.5 * inputs * (1.0 + lax.erf(inputs * HALF_ROOT))

def gelu_slope(inputs):
    return 0.5 * (1.0 + lax.erf(inputs * HALF_ROOT)) + inputs * jnp.exp(-0.5 * inputs * inputs) * BELL_SCALE

def product(left, right):
    return jnp.dot(left, right, preferred_element_type=jnp.float32)

def norm_forward(hidden, norm_gain):
    rounded = round_trip(hidden)
    inv_rms = lax.rsqrt(lax.optimization_barrier(jnp.mean(rounded * rounded, axis=-1, keepdims=True)) + EPSILON)
    normal = rounded * inv_rms
    return ((normal * norm_gain.astype(jnp.float32)).astype(jnp.bfloat16), normal, inv_rms)

def norm_backward(grad_normed, normal, inv_rms, norm_gain):
    grad_normal = grad_normed * norm_gain.astype(jnp.float32)
    grad_hidden = inv_rms * (grad_normal - normal * lax.optimization_barrier(jnp.mean(grad_normal * normal, axis=-1, keepdims=True)))
    return (grad_hidden, lax.optimization_barrier(jnp.sum(grad_normed * normal, axis=0)))

def relative_layout():
    buckets_of = bucket_index(SEQ, BUCKETS)
    distance = np.arange(SEQ)[:, None] - np.arange(SEQ)[None, :]
    return (buckets_of[np.maximum(distance, 0)], distance >= 0)

def bias_matrix(bias_table, index_table):
    return jnp.transpose(bias_table[index_table], (2, 0, 1))

def sequence_scores(queries, key_rows, seg_row, bias_table):
    index_table, causal = relative_layout()
    scores = jnp.einsum('ihd,jhd->hij', queries.astype(jnp.float32), key_rows.astype(jnp.float32)) / math.sqrt(DH)
    scores = scores + bias_matrix(bias_table, index_table)
    allowed = jnp.asarray(causal) & (seg_row[:, None] == seg_row[None, :])
    return jnp.where(allowed[None], scores, NEG_FILL)

def attention_layer(hidden, segments, norm_gain, query_w, key_w, value_w, output_w, bias_w):
    normed, normal, inv_rms = norm_forward(hidden, norm_gain)
    head_shape = (SEQS, SEQ, H, DH)
    query_rows = product(normed, query_w).astype(jnp.bfloat16).reshape(head_shape)
    key_rows = product(normed, key_w).astype(jnp.bfloat16).reshape(head_shape)
    value_rows = product(normed, value_w).astype(jnp.bfloat16).reshape(head_shape)
    bias_table = bias_w.astype(jnp.float32)

    def one_sequence(pack):
        queries, key_seq, value_seq, seg_row = pack
        scores = sequence_scores(queries, key_seq, seg_row, bias_table)
        highest = lax.optimization_barrier(jnp.max(scores, axis=-1, keepdims=True))
        exp_scores = jnp.exp(scores - highest)
        row_total = lax.optimization_barrier(jnp.sum(exp_scores, axis=-1, keepdims=True))
        shares = round_trip(exp_scores / row_total)
        mixed_rows = jnp.einsum('hij,jhd->ihd', shares, value_seq.astype(jnp.float32)).astype(jnp.bfloat16)
        return (mixed_rows, highest[:, :, 0] + jnp.log(row_total[:, :, 0]))
    mixed_rows, log_total = lax.map(one_sequence, (query_rows, key_rows, value_rows, segments))
    mixed_flat = mixed_rows.reshape(TOKENS, H * DH)
    output = hidden + product(mixed_flat, output_w)
    return (output, (normed, normal, inv_rms, query_rows, key_rows, value_rows, mixed_rows, mixed_flat, log_total))

def attention_back(cotangent, saved, segments, norm_gain, query_w, key_w, value_w, output_w, bias_w):
    normed, normal, inv_rms, query_rows, key_rows, value_rows, mixed_rows, mixed_flat, log_total = saved
    grad_low = cotangent.astype(jnp.bfloat16)
    output_grad_w = product(mixed_flat.T, grad_low)
    grad_mixed = product(grad_low, output_w.T).astype(jnp.bfloat16).reshape(SEQS, SEQ, H, DH)
    bias_table = bias_w.astype(jnp.float32)
    index_table, causal = relative_layout()
    inv_root = 1.0 / math.sqrt(DH)

    def one_sequence(pack):
        queries, key_seq, value_seq, seg_row, mixed_seq, log_seq, grad_seq = pack
        scores = sequence_scores(queries, key_seq, seg_row, bias_table)
        shares = jnp.exp(scores - log_seq[:, :, None])
        grad_wide = grad_seq.astype(jnp.float32)
        grad_values = jnp.einsum('hij,ihd->jhd', round_trip(shares), grad_wide).astype(jnp.bfloat16)
        share_grad = jnp.einsum('ihd,jhd->hij', grad_wide, value_seq.astype(jnp.float32))
        row_dot = jnp.einsum('ihd,ihd->hi', grad_wide, mixed_seq.astype(jnp.float32))
        score_grad = shares * (share_grad - row_dot[:, :, None])

        def bias_of(table_in):
            return bias_matrix(table_in, index_table)
        bias_grad = jax.vjp(bias_of, bias_table)[1](score_grad)[0]
        score_low = round_trip(score_grad)
        grad_queries = (jnp.einsum('hij,jhd->ihd', score_low, key_seq.astype(jnp.float32)) * inv_root).astype(jnp.bfloat16)
        grad_keys = (jnp.einsum('hij,ihd->jhd', score_low, queries.astype(jnp.float32)) * inv_root).astype(jnp.bfloat16)
        return (grad_queries, grad_keys, grad_values, bias_grad)
    grad_queries, grad_keys, grad_values, bias_grads = lax.map(one_sequence, (query_rows, key_rows, value_rows, segments, mixed_rows, log_total, grad_mixed))
    grad_queries = grad_queries.reshape(TOKENS, H * DH)
    grad_keys = grad_keys.reshape(TOKENS, H * DH)
    grad_values = grad_values.reshape(TOKENS, H * DH)
    query_grad = product(normed.T, grad_queries)
    key_grad = product(normed.T, grad_keys)
    value_grad = product(normed.T, grad_values)
    grad_normed = product(grad_queries, query_w.T) + product(grad_keys, key_w.T) + product(grad_values, value_w.T)
    grad_hidden, gain_grad = norm_backward(grad_normed, normal, inv_rms, norm_gain)
    return (cotangent + grad_hidden, (gain_grad, query_grad, key_grad, value_grad, output_grad_w, lax.optimization_barrier(jnp.sum(bias_grads, axis=0))))

def dense_layer(hidden, norm_gain, up_w, down_w):
    normed, normal, inv_rms = norm_forward(hidden, norm_gain)
    pre_act = product(normed, up_w)
    active = gelu_value(pre_act).astype(jnp.bfloat16)
    return (hidden + product(active, down_w), (normed, normal, inv_rms, pre_act, active))

def dense_back(cotangent, saved, norm_gain, up_w, down_w):
    normed, normal, inv_rms, pre_act, active = saved
    grad_low = cotangent.astype(jnp.bfloat16)
    down_grad = product(active.T, grad_low)
    grad_pre = (product(grad_low, down_w.T) * gelu_slope(pre_act)).astype(jnp.bfloat16)
    up_grad = product(normed.T, grad_pre)
    grad_normed = product(grad_pre, up_w.T)
    grad_hidden, gain_grad = norm_backward(grad_normed, normal, inv_rms, norm_gain)
    return (cotangent + grad_hidden, gain_grad, up_grad, down_grad)

def slot_plan(route_rows):
    flat_routes = route_rows.reshape(-1)
    onehot = (flat_routes[:, None] == jnp.arange(EXPERTS, dtype=jnp.int32)[None, :]).astype(jnp.int32)
    before = jnp.cumsum(onehot, axis=0) - onehot
    slot_ids = flat_routes * CAP + lax.optimization_barrier(jnp.sum(onehot * before, axis=1))
    slot_owner = jnp.full((EXPERTS * CAP,), SEQ * TOP, jnp.int32).at[slot_ids].set(jnp.arange(SEQ * TOP, dtype=jnp.int32))
    return (slot_ids.reshape(SEQ, TOP), slot_owner)

def take_rows(source_rows, index_rows):
    return source_rows[index_rows]

def to_experts(per_sequence):
    return per_sequence.reshape(SEQS, EXPERTS, CAP, D).transpose(1, 0, 2, 3).reshape(EXPERTS, SEQS * CAP, D)

def to_sequences(per_expert):
    return per_expert.reshape(EXPERTS, SEQS, CAP, D).transpose(1, 0, 2, 3).reshape(SEQS, EXPERTS * CAP, D)

def expert_layer(hidden, routes, gate_weights, norm_gain, expert_up, expert_down):
    normed, normal, inv_rms = norm_forward(hidden, norm_gain)
    slot_ids, slot_owner = jax.vmap(slot_plan)(routes.reshape(SEQS, SEQ, TOP))
    padded = jnp.concatenate([normed.reshape(SEQS, SEQ, D), jnp.zeros((SEQS, 1, D), jnp.bfloat16)], axis=1)
    sent_rows = jax.vmap(take_rows)(padded, slot_owner // TOP)
    by_expert = to_experts(sent_rows)

    def one_expert(pack):
        expert_rows, up_matrix, down_matrix = pack
        active = gelu_value(product(expert_rows, up_matrix)).astype(jnp.bfloat16)
        return product(active, down_matrix)
    outputs = to_sequences(lax.map(one_expert, (by_expert, expert_up, expert_down)))
    picked = jax.vmap(take_rows)(outputs, slot_ids).reshape(TOKENS, TOP, D)
    combined = lax.optimization_barrier(jnp.sum(picked * gate_weights[:, :, None], axis=1))
    return (hidden + combined, (normal, inv_rms, slot_ids, slot_owner, by_expert))

def expert_back(cotangent, saved, gate_weights, norm_gain, expert_up, expert_down):
    normal, inv_rms, slot_ids, slot_owner, by_expert = saved
    scaled = (gate_weights[:, :, None] * round_trip(cotangent)[:, None, :]).astype(jnp.bfloat16)
    padded = jnp.concatenate([scaled.reshape(SEQS, SEQ * TOP, D), jnp.zeros((SEQS, 1, D), jnp.bfloat16)], axis=1)
    grad_by_expert = to_experts(jax.vmap(take_rows)(padded, slot_owner))

    def one_expert(pack):
        expert_rows, grad_rows, up_matrix, down_matrix = pack
        pre_act = product(expert_rows, up_matrix)
        active = gelu_value(pre_act).astype(jnp.bfloat16)
        grad_pre = (product(grad_rows, down_matrix.T) * gelu_slope(pre_act)).astype(jnp.bfloat16)
        return (product(grad_pre, up_matrix.T), product(expert_rows.T, grad_pre), product(active.T, grad_rows))
    grad_inputs, up_grad, down_grad = lax.map(one_expert, (by_expert, grad_by_expert, expert_up, expert_down))
    picked = jax.vmap(take_rows)(to_sequences(grad_inputs), slot_ids).reshape(TOKENS, TOP, D)
    grad_normed = lax.optimization_barrier(jnp.sum(picked, axis=1))
    grad_hidden, gain_grad = norm_backward(grad_normed, normal, inv_rms, norm_gain)
    return (cotangent + grad_hidden, gain_grad, up_grad, down_grad)

def reference(layer_input, segments, routes, gate_weights, first_gain, first_query, first_key, first_value, first_output, first_bias, first_dense_gain, first_dense_up, first_dense_down, second_gain, second_query, second_key, second_value, second_output, second_bias, second_expert_gain, expert_up, expert_down, output_grad):
    hidden_one, saved_one = attention_layer(layer_input, segments, first_gain, first_query, first_key, first_value, first_output, first_bias)
    hidden_two, saved_two = dense_layer(hidden_one, first_dense_gain, first_dense_up, first_dense_down)
    hidden_three, saved_three = attention_layer(hidden_two, segments, second_gain, second_query, second_key, second_value, second_output, second_bias)
    layer_output, saved_four = expert_layer(hidden_three, routes, gate_weights, second_expert_gain, expert_up, expert_down)
    grad_three, expert_gain_grad, expert_up_grad, expert_down_grad = expert_back(output_grad, saved_four, gate_weights, second_expert_gain, expert_up, expert_down)
    grad_two, grads_two = attention_back(grad_three, saved_three, segments, second_gain, second_query, second_key, second_value, second_output, second_bias)
    grad_one, dense_gain_grad, dense_up_grad, dense_down_grad = dense_back(grad_two, saved_two, first_dense_gain, first_dense_up, first_dense_down)
    input_grad, grads_one = attention_back(grad_one, saved_one, segments, first_gain, first_query, first_key, first_value, first_output, first_bias)
    return (layer_output, input_grad, grads_one[0], grads_one[1], grads_one[2], grads_one[3], grads_one[4], grads_one[5], dense_gain_grad, dense_up_grad, dense_down_grad, grads_two[0], grads_two[1], grads_two[2], grads_two[3], grads_two[4], grads_two[5], expert_gain_grad, expert_up_grad, expert_down_grad)
```

```python
import functools
import math

import jax
import jax.numpy as jnp
import numpy as np
from jax import lax
from jax.experimental import pallas as pl
from jax.experimental.pallas import tpu as pltpu
from jax.sharding import PartitionSpec as P

DH = 64
BUCKETS = 32
EPSILON = 1e-06
NEG_FILL = -1e30
HALF_ROOT = 0.7071067811865476
BELL_SCALE = 0.3989422804014327
F32 = jnp.float32
BF16 = jnp.bfloat16


def band_onehot(length, buckets):
    exact_count = buckets // 2
    distance = np.arange(length)
    result = np.minimum(distance, exact_count)
    for bucket_level in range(1, exact_count):
        threshold = int(
            np.ceil(exact_count * (128.0 / exact_count) ** (bucket_level / exact_count))
        )
        result = result + (distance >= threshold)
    band = result[(np.arange(8)[:, None] - np.arange(length)[None, :]) % length]
    return (band.reshape(-1)[:, None] == np.arange(buckets)[None, :]).astype(np.float32)


def band_steps(length, buckets):
    table = band_onehot(length, buckets).reshape(8, length, buckets).transpose(0, 2, 1)
    return np.pad(table, ((0, 0), (0, 128 - buckets), (0, 0)))


def gelu_value(inputs):
    return 0.5 * inputs * (1.0 + lax.erf(inputs * HALF_ROOT))


def gelu_slope(inputs):
    return (
        0.5 * (1.0 + lax.erf(inputs * HALF_ROOT))
        + inputs * jnp.exp(-0.5 * inputs * inputs) * BELL_SCALE
    )


def norm_rows(token_rows, gain_full):
    values = token_rows.astype(F32)
    inv_rms = lax.rsqrt(jnp.mean(values * values, axis=-1, keepdims=True) + EPSILON)
    normal = values * inv_rms
    return ((normal * gain_full).astype(BF16), normal, inv_rms)


def norm_back(grad_normed, normal, inv_rms, gain_full):
    grad_normal = grad_normed * gain_full
    grad_part = inv_rms * (
        grad_normal - normal * jnp.mean(grad_normal * normal, axis=-1, keepdims=True)
    )
    return (grad_part, jnp.sum(grad_normed * normal, axis=0, keepdims=True))


def mm(left, right, left_dim=1, right_dim=0):
    return lax.dot_general(
        left, right, (((left_dim,), (right_dim,)), ((), ())), preferred_element_type=F32
    )


def allowed_pairs(seg_row, seg_col):
    length = seg_row.shape[1]
    rows = lax.broadcasted_iota(jnp.int32, (length, length), 0)
    cols = lax.broadcasted_iota(jnp.int32, (length, length), 1)
    return (rows >= cols) & (seg_row == seg_col)


def head_shares(query, key, band, allowed):
    length = query.shape[0]
    bias = jnp.concatenate(
        [pltpu.roll(band, 8 * step, 1) if step else band for step in range(length // 8)], axis=0
    )
    scores = mm(query, key, 1, 1) * (1.0 / math.sqrt(DH)) + bias
    scores = jnp.where(allowed, scores, NEG_FILL)
    exp_scores = jnp.exp(scores - jnp.max(scores, axis=-1, keepdims=True))
    return exp_scores / jnp.sum(exp_scores, axis=-1, keepdims=True)


def attn_backward_kernel(b_ref, x_ref, g_ref, w_ref, band_ref, segr_ref, segc_ref,
                         qkv_ref, o_ref, wg_ref, part_ref, gain_ref, bandg_ref):
    width = o_ref.shape[1]
    normed, normal, inv_rms = norm_rows(x_ref[...], g_ref[...])
    grad_rows = b_ref[...]
    mixed = o_ref[...]
    qkv = qkv_ref[...]
    weights = w_ref[...]
    grad_mixed = mm(grad_rows, weights[:, 3 * width :]).astype(BF16)
    allowed = allowed_pairs(segr_ref[...], segc_ref[...])
    length = qkv.shape[0]
    inv_root = 1.0 / math.sqrt(DH)
    grad_q, grad_k, grad_v = [], [], []
    for head in range(width // DH):
        lo = head * DH
        query = qkv[:, lo : lo + DH]
        key = qkv[:, width + lo : width + lo + DH]
        value = qkv[:, 2 * width + lo : 2 * width + lo + DH]
        grad_head = grad_mixed[:, lo : lo + DH]
        mixed_head = mixed[:, lo : lo + DH]
        shares = head_shares(query, key, band_ref[head * 8 : head * 8 + 8, :], allowed)
        grad_v.append(mm(shares.astype(BF16), grad_head, 0, 0).astype(BF16))
        row_dot = jnp.sum(
            grad_head.astype(F32) * mixed_head.astype(F32), axis=-1, keepdims=True
        )
        score_grad = shares * (mm(grad_head, value, 1, 1) - row_dot)
        total = score_grad[0:8, :]
        for step in range(1, length // 8):
            total = total + pltpu.roll(
                score_grad[8 * step : 8 * step + 8, :], length - 8 * step, 1
            )
        bandg_ref[head * 8 : head * 8 + 8, :] = total
        score_low = score_grad.astype(BF16)
        grad_q.append((mm(score_low, key) * inv_root).astype(BF16))
        grad_k.append((mm(score_low, query, 0, 0) * inv_root).astype(BF16))
    grad_qkv = jnp.concatenate(grad_q + grad_k + grad_v, axis=1)
    wg_ref[...] = jnp.concatenate(
        [mm(normed, grad_qkv, 0, 0).astype(BF16), mm(grad_rows, mixed, 0, 0).astype(BF16)], axis=1
    )
    grad_normed = mm(grad_qkv, weights[:, : 3 * width], 1, 1)
    grad_part, gain_grad = norm_back(grad_normed, normal, inv_rms, g_ref[...])
    part_ref[...] = grad_part.astype(BF16)
    gain_ref[...] = jnp.broadcast_to(gain_grad, gain_ref.shape)


def dense_backward_kernel(b_ref, x_ref, g_ref, w_ref, pre_ref, up_ref, down_ref, part_ref,
                          gain_ref):
    hidden = pre_ref.shape[1]
    normed, normal, inv_rms = norm_rows(x_ref[...], g_ref[...])
    grad_rows = b_ref[...]
    pre = pre_ref[...]
    active = gelu_value(pre).astype(BF16)
    down_ref[...] = mm(grad_rows, active, 0, 0).astype(BF16)
    grad_pre = (mm(grad_rows, w_ref[:, hidden:]) * gelu_slope(pre)).astype(BF16)
    up_ref[...] = mm(normed, grad_pre, 0, 0).astype(BF16)
    grad_normed = mm(grad_pre, w_ref[:, :hidden], 1, 1)
    grad_part, gain_grad = norm_back(grad_normed, normal, inv_rms, g_ref[...])
    part_ref[...] = grad_part.astype(BF16)
    gain_ref[...] = jnp.broadcast_to(gain_grad, gain_ref.shape)


def call(kernel, outs, *args):
    return pl.pallas_call(
        kernel,
        out_shape=[jax.ShapeDtypeStruct(shape, dtype) for shape, dtype in outs],
        compiler_params=pltpu.CompilerParams(vmem_limit_bytes=40 * 1024 * 1024),
    )(*args)


def greet_peers(count):
    me = lax.axis_index("tensor")
    barrier = pltpu.get_barrier_semaphore()
    for offset in range(1, count):
        pl.semaphore_signal(
            barrier, inc=1, device_id={"tensor": lax.rem(me + offset, count)},
            device_id_type=pl.DeviceIdType.MESH,
        )
    pl.semaphore_wait(barrier, count - 1)
    return me


def remote(source, target, send_sem, recv_sem, peer):
    return pltpu.make_async_remote_copy(
        src_ref=source, dst_ref=target, send_sem=send_sem, recv_sem=recv_sem,
        device_id={"tensor": peer}, device_id_type=pl.DeviceIdType.MESH,
    )


def boundary_kernel(count, with_gain, spread, *refs):
    refs = list(refs)
    part_ref, resid_ref = refs[:2]
    refs = refs[2:]
    gain_ref = refs.pop(0) if with_gain else None
    out_ref = refs.pop(0)
    rows_ref = refs.pop(0) if spread else None
    gain_out = refs.pop(0) if with_gain else None
    land = refs.pop(0)
    gain_land = refs.pop(0) if with_gain else None
    send_sem, recv_sem = refs
    me = greet_peers(count)
    block = out_ref.shape[0]
    own = pl.ds(pl.multiple_of(me * block, block), block)
    copies, gain_copies = [], []
    for offset in range(1, count):
        peer = lax.rem(me + offset, count)
        copy = remote(
            part_ref.at[pl.ds(pl.multiple_of(peer * block, block), block), :],
            land.at[offset - 1], send_sem.at[0, offset], recv_sem.at[0, offset], peer,
        )
        copy.start()
        copies.append(copy)
    if with_gain:
        for offset in range(1, count):
            copy = remote(gain_ref, gain_land.at[offset - 1], send_sem.at[1, offset],
                          recv_sem.at[1, offset], lax.rem(me + offset, count))
            copy.start()
            gain_copies.append(copy)
    total = part_ref[own, :].astype(F32)
    for offset, copy in enumerate(copies):
        copy.wait_recv()
        total = total + land[offset].astype(F32)
    total = resid_ref[...] + total
    out_ref[...] = total
    if spread:
        rows_ref[own, :] = total.astype(BF16)
        for offset in range(1, count):
            copy = remote(rows_ref.at[own, :], rows_ref.at[own, :], send_sem.at[2, offset],
                          recv_sem.at[2, offset], lax.rem(me + offset, count))
            copy.start()
            gain_copies.append(copy)
    for copy in copies:
        copy.wait_send()
    for copy in gain_copies:
        copy.wait()
    if with_gain:
        gain_total = gain_ref[...]
        for offset in range(count - 1):
            gain_total = gain_total + gain_land[offset]
        gain_out[...] = gain_total


def comm_call(kernel, number, outs, scratch, *args):
    vmem = pl.BlockSpec(memory_space=pltpu.VMEM)
    return pl.pallas_call(
        kernel,
        out_shape=[jax.ShapeDtypeStruct(shape, dtype) for shape, dtype in outs],
        in_specs=[vmem] * len(args),
        out_specs=[vmem] * len(outs),
        scratch_shapes=scratch,
        compiler_params=pltpu.CompilerParams(
            collective_id=number, has_side_effects=True, vmem_limit_bytes=40 * 1024 * 1024
        ),
    )(*args)


def boundary(number, part, resid, gain=None, spread=True):
    count = lax.axis_size("tensor")
    block, features = resid.shape
    outs = [((block, features), F32)]
    if spread:
        outs.append((part.shape, BF16))
    scratch = [pltpu.VMEM((count - 1, block, features), BF16)]
    args = [part, resid]
    if gain is not None:
        outs.append((gain.shape, F32))
        scratch.append(pltpu.VMEM((count - 1, *gain.shape), F32))
        args.append(gain)
    scratch += [pltpu.SemaphoreType.DMA((3, count)), pltpu.SemaphoreType.DMA((3, count))]
    return comm_call(
        functools.partial(boundary_kernel, count, gain is not None, spread),
        number, outs, scratch, *args,
    )


def swap_sum(parts, axis_name, count):
    blocks = parts.astype(BF16).reshape(count, parts.shape[0] // count, parts.shape[1])
    arrived = lax.all_to_all(blocks, axis_name, split_axis=0, concat_axis=0, tiled=True)
    return jnp.sum(arrived.astype(F32), axis=0)


def swap_blocks(blocks):
    return lax.all_to_all(blocks, "dp", split_axis=0, concat_axis=0, tiled=True)


def slot_plan(routes, expert_count, capacity):
    length, top_count = routes.shape
    flat_routes = routes.reshape(-1)
    onehot = (flat_routes[:, None] == jnp.arange(expert_count, dtype=jnp.int32)[None, :]).astype(
        BF16
    )
    pairs = jnp.arange(length * top_count, dtype=jnp.int32)
    before = mm((pairs[:, None] > pairs[None, :]).astype(BF16), onehot)
    earlier = jnp.sum(onehot.astype(F32) * before, axis=1).astype(jnp.int32)
    slot_ids = flat_routes * capacity + earlier
    return slot_ids.reshape(length, top_count)


MESH = pl.DeviceIdType.MESH


class Links:
    def __init__(self, send_sem, recv_sem):
        self.send_sem, self.recv_sem = send_sem, recv_sem
        self.copies = []

    def push(self, source, target, where):
        index = len(self.copies)
        copy = pltpu.make_async_remote_copy(
            src_ref=source, dst_ref=target, send_sem=self.send_sem.at[index],
            recv_sem=self.recv_sem.at[index], device_id=where, device_id_type=MESH,
        )
        copy.start()
        self.copies.append(copy)
        return copy

    def finish(self):
        for copy in self.copies:
            copy.wait_send()


class Place:
    def __init__(self, dp_count, tensor_count):
        self.dp_count, self.tensor_count = dp_count, tensor_count
        self.groups = dp_count // 2
        self.dp = lax.axis_index("dp")
        self.rank = lax.axis_index("tensor")
        self.side = lax.rem(self.dp, 2)
        self.group = lax.div(self.dp, 2)
        self.twin = {"dp": self.dp + 1 - 2 * self.side}

    def rank_at(self, offset):
        return lax.rem(self.rank + offset, self.tensor_count)

    def group_at(self, offset):
        return lax.rem(self.group + offset, self.groups)

    def dp_at(self, offset):
        return lax.rem(self.dp + offset, self.dp_count)

    def greet(self):
        barrier = pltpu.get_barrier_semaphore()
        partners = [{"tensor": self.rank_at(o)} for o in range(1, self.tensor_count)]
        partners += [{"dp": self.dp_at(o)} for o in range(1, self.dp_count)]
        for partner in partners:
            pl.semaphore_signal(barrier, inc=1, device_id=partner, device_id_type=MESH)
        pl.semaphore_wait(barrier, len(partners))

    def own_rows(self, block):
        return pl.ds(pl.multiple_of(self.rank * block, block), block)


def wait_all(copies):
    for copy in copies:
        copy.wait_recv()


def spread_rows(links, place, rows_ref, block):
    own = place.own_rows(block)
    return [
        links.push(rows_ref.at[own, :], rows_ref.at[own, :], {"tensor": place.rank_at(offset)})
        for offset in range(1, place.tensor_count)
    ]


def scatter_rows(links, place, part_ref, land_ref, block):
    copies = []
    for offset in range(1, place.tensor_count):
        peer = place.rank_at(offset)
        rows = pl.ds(pl.multiple_of(peer * block, block), block)
        copies.append(
            links.push(part_ref.at[rows, :], land_ref.at[offset - 1], {"tensor": peer})
        )
    return copies


def take_rows(place, copies, part_ref, land_ref, block):
    total = part_ref[place.own_rows(block), :].astype(F32)
    for offset, copy in enumerate(copies):
        copy.wait_recv()
        total = total + land_ref[offset].astype(F32)
    return total


def gather_start(links, place, source_ref, full_ref):
    first = links.push(source_ref, full_ref.at[place.dp], place.twin)
    full_ref[place.dp] = source_ref[...]
    others = [
        links.push(
            source_ref, full_ref.at[place.dp],
            {"dp": place.group_at(offset) * 2 + place.side},
        )
        for offset in range(1, place.groups)
    ]
    return first, others


def gather_forward(links, place, started, full_ref):
    first, others = started
    passed = [first]
    for offset, copy in enumerate(others, 1):
        copy.wait_recv()
        origin = place.group_at(place.groups - offset) * 2 + place.side
        passed.append(links.push(full_ref.at[origin], full_ref.at[origin], place.twin))
    return passed


def swap_start(links, place, sent_ref, arrived_ref):
    copies = []
    for offset in range(1, place.dp_count):
        peer = place.dp_at(offset)
        copies.append(links.push(sent_ref.at[peer], arrived_ref.at[place.dp], {"dp": peer}))
    arrived_ref[place.dp] = sent_ref[place.dp]
    return copies


def flat(ref):
    count, rows, columns = ref.shape
    return ref[...].reshape(count * rows, columns)


def attn_forward(x_rows, gain, weights, band_ref, allowed, qkv_ref, o_ref, part_ref):
    normed, _, _ = norm_rows(x_rows, gain)
    width = o_ref.shape[1]
    qkv = mm(normed, weights[:, : 3 * width]).astype(BF16)
    qkv_ref[...] = qkv
    mixed = []
    for head in range(width // DH):
        lo = head * DH
        shares = head_shares(
            qkv[:, lo : lo + DH],
            qkv[:, width + lo : width + lo + DH],
            band_ref[head * 8 : head * 8 + 8, :],
            allowed,
        ).astype(BF16)
        mixed.append(mm(shares, qkv[:, 2 * width + lo : 2 * width + lo + DH]).astype(BF16))
    mixed = jnp.concatenate(mixed, axis=1)
    o_ref[...] = mixed
    part_ref[...] = mm(mixed, weights[:, 3 * width :], 1, 1).astype(BF16)


def slot_places(slots, slot_row):
    shape = (slots, slot_row.shape[1])
    return lax.broadcasted_iota(jnp.int32, shape, 0) == slot_row


def make_bands(biases, onehot_ref, band_refs, heads):
    length = onehot_ref.shape[2]
    for layer, band_ref in enumerate(band_refs):
        block = biases[:, layer * 128 : layer * 128 + 128].astype(BF16)
        rows = [mm(block, onehot_ref[step]) for step in range(8)]
        for head in range(heads):
            band_ref[head * 8 : head * 8 + 8, :] = jnp.concatenate(
                [row[head : head + 1, :] for row in rows], axis=0
            )


def forward_kernel(
    dp_count, tensor_count,
    x_ref, og_ref, small_ref, w1_ref, wd_ref, w2_ref, segr_ref, segc_ref, slot_ref, gate_ref,
    onehot_ref,
    rows0_ref, rows1_ref, rows2_ref, rows3_ref, x3_ref, gains_ref, band1_ref, band2_ref,
    w1f_ref, wdf_ref, w2f_ref, qkv1_ref, o1_ref, qkv2_ref, o2_ref, pre_ref, arr_ref, arrg_ref,
    ogr_ref, part_ref, land_ref, small_land, small_full, sent_ref, sentg_ref, send_sem, recv_sem,
):
    place = Place(dp_count, tensor_count)
    links = Links(send_sem, recv_sem)
    block, features = x_ref.shape
    length = rows0_ref.shape[0]
    heads = band1_ref.shape[0] // 8
    own = place.own_rows(block)
    rows0_ref[own, :] = x_ref[...].astype(BF16)
    ogr_ref[own, :] = og_ref[...].astype(BF16)
    place.greet()

    small_land[place.rank] = small_ref[...]
    small_z = [
        links.push(small_ref, small_land.at[place.rank], {"tensor": place.rank_at(offset)})
        for offset in range(1, tensor_count)
    ]
    x_copies = spread_rows(links, place, rows0_ref, block)
    one_started = gather_start(links, place, w1_ref, w1f_ref)
    wait_all(small_z)
    gains = small_land[0, 0:8, :].astype(F32)
    for rank in range(1, tensor_count):
        gains = gains + small_land[rank, 0:8, :].astype(F32)
    small_full[place.dp] = jnp.concatenate(
        [gains, small_ref[8:16, :].astype(F32)], axis=0
    ).astype(BF16)
    small_dp = [
        links.push(small_full.at[place.dp], small_full.at[place.dp], {"dp": place.dp_at(offset)})
        for offset in range(1, dp_count)
    ]
    og_copies = spread_rows(links, place, ogr_ref, block)
    one_passed = gather_forward(links, place, one_started, w1f_ref)
    dense_started = gather_start(links, place, wd_ref, wdf_ref)
    allowed = allowed_pairs(segr_ref[...], segc_ref[...])
    wait_all(small_dp)
    smalls = small_full[0].astype(F32)
    for peer in range(1, dp_count):
        smalls = smalls + small_full[peer].astype(F32)
    gains_ref[...] = smalls[0:8, :]
    make_bands(smalls[8:16, :], onehot_ref, (band1_ref, band2_ref), heads)
    wait_all(x_copies)
    wait_all(one_passed)

    attn_forward(rows0_ref[...], gains_ref[0:1, :], flat(w1f_ref), band1_ref, allowed,
                 qkv1_ref, o1_ref, part_ref.at[0])
    copies = scatter_rows(links, place, part_ref.at[0], land_ref.at[0], block)
    wait_all(og_copies)
    slots = sent_ref.shape[0] * sent_ref.shape[1]
    out_rows = ogr_ref[...].astype(F32)
    scaled = jnp.concatenate(
        [(gate_ref[:, c : c + 1] * out_rows).astype(BF16) for c in range(gate_ref.shape[1])],
        axis=0,
    )
    chosen = slot_places(slots, slot_ref[...])
    sentg_ref[...] = mm(chosen.astype(BF16), scaled).astype(BF16).reshape(sentg_ref.shape)
    total = x_ref[...] + take_rows(place, copies, part_ref.at[0], land_ref.at[0], block)
    rows1_ref[own, :] = total.astype(BF16)
    copies = spread_rows(links, place, rows1_ref, block)
    dense_passed = gather_forward(links, place, dense_started, wdf_ref)
    two_started = gather_start(links, place, w2_ref, w2f_ref)
    wait_all(copies)
    wait_all(dense_passed)

    hidden = pre_ref.shape[1]
    normed, _, _ = norm_rows(rows1_ref[...], gains_ref[1:2, :])
    weights = flat(wdf_ref)
    pre = mm(normed, weights[:, :hidden])
    pre_ref[...] = pre
    part_ref[1] = mm(gelu_value(pre).astype(BF16), weights[:, hidden:], 1, 1).astype(BF16)
    copies = scatter_rows(links, place, part_ref.at[1], land_ref.at[1], block)
    two_passed = gather_forward(links, place, two_started, w2f_ref)
    arrg_copies = swap_start(links, place, sentg_ref, arrg_ref)
    total = total + take_rows(place, copies, part_ref.at[1], land_ref.at[1], block)
    rows2_ref[own, :] = total.astype(BF16)
    copies = spread_rows(links, place, rows2_ref, block)
    wait_all(copies)
    wait_all(two_passed)

    attn_forward(rows2_ref[...], gains_ref[2:3, :], flat(w2f_ref), band2_ref, allowed,
                 qkv2_ref, o2_ref, part_ref.at[2])
    copies = scatter_rows(links, place, part_ref.at[2], land_ref.at[2], block)
    total = total + take_rows(place, copies, part_ref.at[2], land_ref.at[2], block)
    x3_ref[...] = total
    rows3_ref[own, :] = total.astype(BF16)
    copies = spread_rows(links, place, rows3_ref, block)
    chosen_rows = slot_places(slots, slot_ref[:, :length]) | slot_places(
        slots, slot_ref[:, length:]
    )
    chosen_rows = chosen_rows.astype(BF16)
    wait_all(copies)
    normed, _, _ = norm_rows(rows3_ref[...], gains_ref[3:4, :])
    sent_ref[...] = mm(chosen_rows, normed).astype(BF16).reshape(sent_ref.shape)
    arr_copies = swap_start(links, place, sent_ref, arr_ref)
    wait_all(arrg_copies)
    wait_all(arr_copies)
    links.finish()


def on_device(
    layer_input, segments, routes, gate_weights,
    first_gain, first_query, first_key, first_value, first_output, first_bias,
    first_dense_gain, first_dense_up, first_dense_down,
    second_gain, second_query, second_key, second_value, second_output, second_bias,
    second_expert_gain, expert_up, expert_down, output_grad,
):
    dp_count, tensor_count = lax.axis_size("dp"), lax.axis_size("tensor")
    tensor_index = lax.axis_index("tensor")
    length = segments.shape[1]
    features = layer_input.shape[1]
    width = first_query.shape[1]
    heads = first_bias.shape[1]
    hidden = first_dense_up.shape[1]
    piece = first_gain.shape[0]
    bias_rows = first_bias.shape[0]
    table = jnp.asarray(band_onehot(length, BUCKETS))

    dp_index = lax.axis_index("dp")
    own_gains = jnp.stack([first_gain, first_dense_gain, second_gain, second_expert_gain])
    small = jnp.zeros((16, features), BF16)
    small = lax.dynamic_update_slice(
        small, own_gains, (0, (dp_index * tensor_count + tensor_index) * piece)
    )
    for layer, bias in enumerate((first_bias, second_bias)):
        small = lax.dynamic_update_slice(
            small, bias.T, (8, layer * 128 + dp_index * bias_rows)
        )
    pad = (-(4 * piece + 2 * bias_rows * heads)) % 128

    one_own = jnp.concatenate([first_query, first_key, first_value, first_output.T], axis=1)
    dense_own = jnp.concatenate([first_dense_up, first_dense_down.T], axis=1)
    two_own = jnp.concatenate([second_query, second_key, second_value, second_output.T], axis=1)
    seg_row = segments
    seg_col = segments.reshape(length, 1)

    def attn_backward(grad_rows, saved):
        x_rows, gain, weights, band, qkv, mixed = saved
        return call(
            attn_backward_kernel,
            [((features, 4 * width), BF16), ((length, features), BF16), ((8, features), F32),
             ((heads * 8, length), F32)],
            grad_rows, x_rows, gain, weights, band, seg_row, seg_col, qkv, mixed,
        )

    top_count = routes.shape[1]
    local_experts = expert_up.shape[0]
    expert_count = local_experts * dp_count
    capacity = max(2, 3 * length * top_count // (2 * expert_count))
    capacity = -(-capacity // 16) * 16
    slots = expert_count * capacity
    slot_ids = slot_plan(routes, expert_count, capacity)
    slot_flat = slot_ids.T.reshape(1, top_count * length)
    place = (jnp.arange(slots, dtype=jnp.int32)[:, None] == slot_flat).astype(BF16)
    place_rows = place.reshape(slots, top_count, length).sum(axis=1)
    sent_shape = (dp_count, local_experts, capacity, features)
    swap_shape = (dp_count, local_experts * capacity, features)
    weight_rows = first_query.shape[0]
    block = layer_input.shape[0]
    rows_shape = ((length, features), BF16)
    wide = 4 * width
    outs = [
        rows_shape, rows_shape, rows_shape, rows_shape, ((block, features), F32),
        ((8, features), F32), ((heads * 8, length), F32), ((heads * 8, length), F32),
        ((dp_count, weight_rows, wide), BF16), ((dp_count, weight_rows, 2 * hidden), BF16),
        ((dp_count, weight_rows, wide), BF16),
        ((length, 3 * width), BF16), ((length, width), BF16),
        ((length, 3 * width), BF16), ((length, width), BF16),
        ((length, hidden), F32), (swap_shape, BF16), (swap_shape, BF16),
    ]
    copies = 8 * tensor_count + 8 * dp_count
    scratch = [
        pltpu.VMEM((length, features), BF16),
        pltpu.VMEM((3, length, features), BF16),
        pltpu.VMEM((3, tensor_count - 1, block, features), BF16),
        pltpu.VMEM((tensor_count, 16, features), BF16),
        pltpu.VMEM((dp_count, 16, features), BF16),
        pltpu.VMEM(swap_shape, BF16),
        pltpu.VMEM(swap_shape, BF16),
        pltpu.SemaphoreType.DMA((copies,)),
        pltpu.SemaphoreType.DMA((copies,)),
    ]
    (
        rows_zero, rows_one, rows_two, rows_three, hidden_three, gains_full, band_one, band_two,
        weights_one, weights_dense, weights_two, qkv_one, mixed_one, qkv_two, mixed_two,
        pre_act, arrived, arrived_grad,
    ) = comm_call(
        functools.partial(forward_kernel, dp_count, tensor_count), 1, outs, scratch,
        layer_input, output_grad, small, one_own, dense_own, two_own, seg_row, seg_col,
        slot_flat, gate_weights, jnp.asarray(band_steps(length, BUCKETS), BF16),
    )
    weights_one = weights_one.reshape(-1, wide)
    weights_two = weights_two.reshape(-1, wide)
    weights_dense = weights_dense.reshape(-1, 2 * hidden)
    gains = [gains_full[k : k + 1] for k in range(4)]
    saved_one = (rows_zero, gains[0], weights_one, band_one, qkv_one, mixed_one)
    saved_three = (rows_two, gains[2], weights_two, band_two, qkv_two, mixed_two)
    arrived = arrived.reshape(sent_shape)
    arrived_grad = arrived_grad.reshape(sent_shape)
    normed, normal, inv_rms = norm_rows(rows_three, gains[3])
    pre_expert = jnp.einsum("secd,edf->secf", arrived, expert_up, preferred_element_type=F32)

    grad_active = jnp.einsum(
        "secd,efd->secf", arrived_grad, expert_down, preferred_element_type=F32
    )
    grad_pre = (grad_active * gelu_slope(pre_expert)).astype(BF16)
    grad_sent = jnp.einsum(
        "secf,edf->secd", grad_pre, expert_up, preferred_element_type=F32
    ).astype(BF16)
    grad_back = swap_blocks(grad_sent).reshape(slots, features)
    grad_normed = mm(place_rows, grad_back, 0, 0)
    grad_part, expert_gain_grad = norm_back(grad_normed, normal, inv_rms, gains[3])
    grad_three, grad_rows_three, gain_expert = boundary(
        3, grad_part.astype(BF16), output_grad,
        jnp.broadcast_to(expert_gain_grad, (8, features)),
    )

    active = gelu_value(pre_expert).astype(BF16)
    expert_rows = jnp.einsum(
        "secf,efd->secd", active, expert_down, preferred_element_type=F32
    ).astype(BF16)
    returned = swap_blocks(expert_rows).reshape(slots, features)
    picked = mm(place, returned, 0, 0).reshape(top_count, length, features)
    combined = jnp.sum(picked * gate_weights.T[:, :, None], axis=0)
    (layer_output,) = boundary(4, combined.astype(BF16), hidden_three, spread=False)
    expert_down_grad = jnp.einsum("secf,secd->efd", active, arrived_grad, preferred_element_type=F32)
    expert_up_grad = jnp.einsum("secd,secf->edf", arrived, grad_pre, preferred_element_type=F32)

    wg_two, part, gain_two, band_grad_two = attn_backward(grad_rows_three, saved_three)
    summed_two = swap_sum(wg_two, "dp", dp_count)
    grad_two, grad_rows_two, gain_two = boundary(3, part, grad_three, gain_two)
    up_wg, down_wg, part, gain_dense = call(
        dense_backward_kernel,
        [((features, hidden), BF16), ((features, hidden), BF16), ((length, features), BF16),
         ((8, features), F32)],
        grad_rows_two, rows_one, gains[1], weights_dense, pre_act,
    )
    dense_up_grad = swap_sum(up_wg, "dp", dp_count)
    dense_down_grad = swap_sum(down_wg, "dp", dp_count).T
    grad_one, grad_rows_one, gain_dense = boundary(3, part, grad_two, gain_dense)
    wg_one, part, gain_one, band_grad_one = attn_backward(grad_rows_one, saved_one)
    summed_one = swap_sum(wg_one, "dp", dp_count)
    grad_zero, gain_one = boundary(5, part, grad_one, gain_one, spread=False)

    def bias_block(band_grad):
        grad = jnp.dot(
            table.T, band_grad.reshape(heads, 8 * length).T, precision=lax.Precision.HIGHEST
        )
        return grad.reshape(dp_count, bias_rows * heads)

    def gain_block(gain_sum):
        block = gain_sum[0].reshape(dp_count, tensor_count, piece)
        return lax.dynamic_index_in_dim(block, tensor_index, 1, keepdims=False)

    sent_small = jnp.concatenate(
        [gain_block(gain) for gain in (gain_one, gain_dense, gain_two, gain_expert)]
        + [bias_block(band_grad_one), bias_block(band_grad_two)],
        axis=1,
    )
    sent_small = jnp.pad(sent_small, ((0, 0), (0, pad)))
    totals = jnp.sum(
        lax.all_to_all(sent_small, "dp", split_axis=0, concat_axis=0, tiled=True), axis=0
    )
    gain_grads = [totals[k * piece : (k + 1) * piece] for k in range(4)]
    bias_grads = [
        totals[4 * piece + k * bias_rows * heads :][: bias_rows * heads].reshape(bias_rows, heads)
        for k in range(2)
    ]

    def split_four(summed):
        return (
            summed[:, :width],
            summed[:, width : 2 * width],
            summed[:, 2 * width : 3 * width],
            summed[:, 3 * width :].T,
        )

    return (
        layer_output,
        grad_zero,
        gain_grads[0],
        *split_four(summed_one),
        bias_grads[0],
        gain_grads[1],
        dense_up_grad,
        dense_down_grad,
        gain_grads[2],
        *split_four(summed_two),
        bias_grads[1],
        gain_grads[3],
        expert_up_grad,
        expert_down_grad,
    )


def solution(mesh):
    attn = (P("dp", "tensor"), P("dp", "tensor"), P("dp", "tensor"), P("tensor", "dp"),
            P("dp", "tensor"))
    both = P(("dp", "tensor"))
    rows = P(("dp", "tensor"), None)
    return jax.shard_map(
        on_device,
        mesh=mesh,
        in_specs=(
            rows, P("dp", None), P("dp", None), P("dp", None),
            both, *attn,
            both, P("dp", "tensor"), P("tensor", "dp"),
            both, *attn,
            both, P("dp", None, "tensor"), P("dp", "tensor", None), rows,
        ),
        out_specs=(
            rows, rows,
            both, *attn,
            both, P("dp", "tensor"), P("tensor", "dp"),
            both, *attn,
            both, P("dp", None, "tensor"), P("dp", "tensor", None),
        ),
        check_vma=False,
    )
```

```python
import functools
import math

import jax
import jax.numpy as jnp
import numpy as np
from jax import lax
from jax.experimental import pallas as pl
from jax.experimental.pallas import tpu as pltpu
from jax.sharding import PartitionSpec as P

DH = 64
BUCKETS = 32
EPSILON = 1e-06
NEG_FILL = -1e30
HALF_ROOT = 0.7071067811865476
BELL_SCALE = 0.3989422804014327
F32 = jnp.float32
BF16 = jnp.bfloat16
PIECES = 2


def band_onehot(length, buckets):
    exact_count = buckets // 2
    distance = np.arange(length)
    result = np.minimum(distance, exact_count)
    for bucket_level in range(1, exact_count):
        threshold = int(
            np.ceil(exact_count * (128.0 / exact_count) ** (bucket_level / exact_count))
        )
        result = result + (distance >= threshold)
    band = result[(np.arange(8)[:, None] - np.arange(length)[None, :]) % length]
    return (band.reshape(-1)[:, None] == np.arange(buckets)[None, :]).astype(np.float32)


def band_steps(length, buckets):
    table = band_onehot(length, buckets).reshape(8, length, buckets).transpose(0, 2, 1)
    return np.pad(table, ((0, 0), (0, 128 - buckets), (0, 0)))


def gelu_value(inputs):
    return 0.5 * inputs * (1.0 + lax.erf(inputs * HALF_ROOT))


def gelu_slope(inputs):
    return (
        0.5 * (1.0 + lax.erf(inputs * HALF_ROOT))
        + inputs * jnp.exp(-0.5 * inputs * inputs) * BELL_SCALE
    )


def norm_rows(token_rows, gain_full):
    values = token_rows.astype(F32)
    inv_rms = lax.rsqrt(jnp.mean(values * values, axis=-1, keepdims=True) + EPSILON)
    normal = values * inv_rms
    return ((normal * gain_full).astype(BF16), normal, inv_rms)


def norm_back(grad_normed, normal, inv_rms, gain_full):
    grad_normal = grad_normed * gain_full
    grad_part = inv_rms * (
        grad_normal - normal * jnp.mean(grad_normal * normal, axis=-1, keepdims=True)
    )
    return (grad_part, jnp.sum(grad_normed * normal, axis=0, keepdims=True))


def mm(left, right, left_dim=1, right_dim=0):
    return lax.dot_general(
        left, right, (((left_dim,), (right_dim,)), ((), ())), preferred_element_type=F32
    )


def allowed_pairs(seg_row, seg_col):
    length = seg_row.shape[1]
    rows = lax.broadcasted_iota(jnp.int32, (length, length), 0)
    cols = lax.broadcasted_iota(jnp.int32, (length, length), 1)
    return (rows >= cols) & (seg_row == seg_col)


def head_shares(query, key, band, allowed):
    length = query.shape[0]
    bias = jnp.concatenate(
        [pltpu.roll(band, 8 * step, 1) if step else band for step in range(length // 8)], axis=0
    )
    scores = mm(query, key, 1, 1) * (1.0 / math.sqrt(DH)) + bias
    scores = jnp.where(allowed, scores, NEG_FILL)
    exp_scores = jnp.exp(scores - jnp.max(scores, axis=-1, keepdims=True))
    return exp_scores / jnp.sum(exp_scores, axis=-1, keepdims=True)


MESH = pl.DeviceIdType.MESH


class Links:
    def __init__(self, send_sem, recv_sem):
        self.send_sem, self.recv_sem = send_sem, recv_sem
        self.copies = []

    def push(self, source, target, where):
        index = len(self.copies)
        copy = pltpu.make_async_remote_copy(
            src_ref=source, dst_ref=target, send_sem=self.send_sem.at[index],
            recv_sem=self.recv_sem.at[index], device_id=where, device_id_type=MESH,
        )
        copy.start()
        self.copies.append(copy)
        return copy

    def finish(self):
        for copy in self.copies:
            copy.wait_send()


class Place:
    def __init__(self, dp_count, tensor_count):
        self.dp_count, self.tensor_count = dp_count, tensor_count
        self.groups = dp_count // 2
        self.dp = lax.axis_index("dp")
        self.rank = lax.axis_index("tensor")
        self.side = lax.rem(self.dp, 2)
        self.group = lax.div(self.dp, 2)
        self.twin = {"dp": self.dp + 1 - 2 * self.side}

    def rank_at(self, offset):
        return lax.rem(self.rank + offset, self.tensor_count)

    def group_at(self, offset):
        return lax.rem(self.group + offset, self.groups)

    def dp_at(self, offset):
        return lax.rem(self.dp + offset, self.dp_count)

    def greet(self):
        barrier = pltpu.get_barrier_semaphore()
        partners = [{"tensor": self.rank_at(o)} for o in range(1, self.tensor_count)]
        partners += [{"dp": self.dp_at(o)} for o in range(1, self.dp_count)]
        for partner in partners:
            pl.semaphore_signal(barrier, inc=1, device_id=partner, device_id_type=MESH)

    def met(self):
        pl.semaphore_wait(
            pltpu.get_barrier_semaphore(), self.tensor_count + self.dp_count - 2
        )

    def own_rows(self, block):
        return pl.ds(pl.multiple_of(self.rank * block, block), block)


def wait_all(copies):
    for copy in copies:
        copy.wait_recv()


def spread_rows(links, place, rows_ref, block):
    own = place.own_rows(block)
    return [
        links.push(rows_ref.at[own, :], rows_ref.at[own, :], {"tensor": place.rank_at(offset)})
        for offset in range(1, place.tensor_count)
    ]


def piece_rows(start, block, piece):
    size = block // PIECES
    return pl.ds(pl.multiple_of(start + piece * size, size), size)


def scatter_rows(links, place, part_ref, land_ref, block):
    pieces = []
    for piece in range(PIECES):
        copies = []
        for offset in range(1, place.tensor_count):
            peer = place.rank_at(offset)
            copies.append(
                links.push(
                    part_ref.at[piece_rows(peer * block, block, piece), :],
                    land_ref.at[offset - 1, piece_rows(0, block, piece)], {"tensor": peer},
                )
            )
        pieces.append(copies)
    return pieces


def settle(links, place, pieces, part_ref, land_ref, resid, rows_ref=None):
    block = land_ref.shape[1]
    totals, spread = [], []
    for piece, copies in enumerate(pieces):
        own = piece_rows(place.rank * block, block, piece)
        total = part_ref[own, :].astype(F32)
        for offset, copy in enumerate(copies):
            copy.wait_recv()
            total = total + land_ref[offset, piece_rows(0, block, piece)].astype(F32)
        total = resid[piece] + total
        totals.append(total)
        if rows_ref is not None:
            rows_ref[own, :] = total.astype(BF16)
            for offset in range(1, place.tensor_count):
                spread.append(
                    links.push(
                        rows_ref.at[own, :], rows_ref.at[own, :],
                        {"tensor": place.rank_at(offset)},
                    )
                )
    return totals, spread


def cut(ref):
    block = ref.shape[0]
    return [ref[piece_rows(0, block, piece), :] for piece in range(PIECES)]


def gather_start(links, place, full_ref):
    first = links.push(full_ref.at[place.dp], full_ref.at[place.dp], place.twin)
    others = [
        links.push(
            full_ref.at[place.dp], full_ref.at[place.dp],
            {"dp": place.group_at(offset) * 2 + place.side},
        )
        for offset in range(1, place.groups)
    ]
    return first, others


def gather_forward(links, place, started, full_ref):
    first, others = started
    passed = [first]
    for offset, copy in enumerate(others, 1):
        copy.wait_recv()
        origin = place.group_at(place.groups - offset) * 2 + place.side
        passed.append(links.push(full_ref.at[origin], full_ref.at[origin], place.twin))
    return passed


def swap_start(links, place, sent_ref, arrived_ref, part):
    copies = []
    for offset in range(1, place.dp_count):
        peer = place.dp_at(offset)
        copies.append(
            links.push(sent_ref.at[part, peer], arrived_ref.at[part, place.dp], {"dp": peer})
        )
    arrived_ref[part, place.dp] = sent_ref[part, place.dp]
    return copies


def flat(ref):
    count, rows, columns = ref.shape
    return ref[...].reshape(count * rows, columns)


def attn_forward(x_rows, gain, weights, band_ref, allowed, qkv_ref, o_ref, part_ref):
    normed, _, _ = norm_rows(x_rows, gain)
    width = o_ref.shape[1]
    qkv = mm(normed, weights[:, : 3 * width]).astype(BF16)
    qkv_ref[...] = qkv
    mixed = []
    for head in range(width // DH):
        lo = head * DH
        shares = head_shares(
            qkv[:, lo : lo + DH],
            qkv[:, width + lo : width + lo + DH],
            band_ref[head * 8 : head * 8 + 8, :],
            allowed,
        ).astype(BF16)
        mixed.append(mm(shares, qkv[:, 2 * width + lo : 2 * width + lo + DH]).astype(BF16))
    mixed = jnp.concatenate(mixed, axis=1)
    o_ref[...] = mixed
    part_ref[...] = mm(mixed, weights[:, 3 * width :], 1, 1).astype(BF16)


def slot_places(slots, slot_row):
    shape = (slots, slot_row.shape[1])
    return lax.broadcasted_iota(jnp.int32, shape, 0) == slot_row


def slot_rows(routes_ref, dp_count, experts, capacity):
    top_count, length = routes_ref.shape
    named = []
    for c in range(top_count):
        row = routes_ref[c : c + 1, :]
        first = lax.broadcasted_iota(jnp.int32, (dp_count, length), 0) * experts
        named.append(
            jnp.concatenate(
                [jnp.where(first + e == row, 1.0, 0.0) for e in range(experts)], axis=0
            )
        )
    total = named[0]
    for one in named[1:]:
        total = total + one
    shape = (length, length)
    earlier = lax.broadcasted_iota(jnp.int32, shape, 0) < lax.broadcasted_iota(jnp.int32, shape, 1)
    before = mm(total.astype(BF16), jnp.where(earlier, 1.0, 0.0).astype(BF16))
    start = lax.broadcasted_iota(jnp.int32, before.shape, 0).astype(F32) * capacity
    return [jnp.sum(one * (start + before), axis=0, keepdims=True) for one in named]


def place_values(count, start, columns):
    shape = (count, columns)
    rows = lax.broadcasted_iota(jnp.int32, shape, 0)
    target = rows + start == lax.broadcasted_iota(jnp.int32, shape, 1)
    return jnp.where(target, 1.0, 0.0).astype(BF16)


def make_bands(biases, onehot_ref, band_refs, heads):
    length = onehot_ref.shape[2]
    for layer, band_ref in enumerate(band_refs):
        block = biases[:, layer * 128 : layer * 128 + 128].astype(BF16)
        rows = [mm(block, onehot_ref[step]) for step in range(8)]
        for head in range(heads):
            band_ref[head * 8 : head * 8 + 8, :] = jnp.concatenate(
                [row[head : head + 1, :] for row in rows], axis=0
            )


def attn_backward(grad_rows, x_rows, gain, weights, band_ref, allowed, qkv_ref, o_ref,
                  part_ref, gain_ref, bandg_ref):
    width = o_ref.shape[1]
    normed, normal, inv_rms = norm_rows(x_rows, gain)
    mixed = o_ref[...]
    qkv = qkv_ref[...]
    grad_mixed = mm(grad_rows, weights[:, 3 * width :]).astype(BF16)
    length = qkv.shape[0]
    inv_root = 1.0 / math.sqrt(DH)
    grad_q, grad_k, grad_v = [], [], []
    for head in range(width // DH):
        lo = head * DH
        query = qkv[:, lo : lo + DH]
        key = qkv[:, width + lo : width + lo + DH]
        value = qkv[:, 2 * width + lo : 2 * width + lo + DH]
        grad_head = grad_mixed[:, lo : lo + DH]
        mixed_head = mixed[:, lo : lo + DH]
        shares = head_shares(query, key, band_ref[head * 8 : head * 8 + 8, :], allowed)
        grad_v.append(mm(shares.astype(BF16), grad_head, 0, 0).astype(BF16))
        row_dot = jnp.sum(
            grad_head.astype(F32) * mixed_head.astype(F32), axis=-1, keepdims=True
        )
        score_grad = shares * (mm(grad_head, value, 1, 1) - row_dot)
        total = score_grad[0:8, :]
        for step in range(1, length // 8):
            total = total + pltpu.roll(
                score_grad[8 * step : 8 * step + 8, :], length - 8 * step, 1
            )
        bandg_ref[head * 8 : head * 8 + 8, :] = total
        score_low = score_grad.astype(BF16)
        grad_q.append((mm(score_low, key) * inv_root).astype(BF16))
        grad_k.append((mm(score_low, query, 0, 0) * inv_root).astype(BF16))
    grad_qkv = jnp.concatenate(grad_q + grad_k + grad_v, axis=1)
    grad_normed = mm(grad_qkv, weights[:, : 3 * width], 1, 1)
    grad_part, gain_grad = norm_back(grad_normed, normal, inv_rms, gain)
    part_ref[...] = grad_part.astype(BF16)
    gain_ref[...] = gain_grad
    return normed, grad_qkv, mixed


def attn_weights_grad(grad_rows, kept, wg_ref):
    normed, grad_qkv, mixed = kept
    wg = jnp.concatenate(
        [mm(normed, grad_qkv, 0, 0).astype(BF16), mm(grad_rows, mixed, 0, 0).astype(BF16)], axis=1
    )
    wg_ref[...] = wg.reshape(wg_ref.shape)


def sum_start(links, place, wg_ref, pair_ref):
    return links.push(wg_ref.at[:, 1 - place.side], pair_ref, place.twin)


def sum_onward(links, place, started, wg_ref, pair_ref, out_ref):
    started.wait_recv()
    pair_ref[...] = (
        wg_ref[:, place.side].astype(F32) + pair_ref[...].astype(F32)
    ).astype(BF16)
    copies = []
    for offset in range(1, place.groups):
        peer = place.group_at(offset)
        copies.append(
            links.push(pair_ref.at[peer], out_ref.at[offset], {"dp": peer * 2 + place.side})
        )
    out_ref[0] = pair_ref[place.group]
    return copies


def bias_sums(bandg_ref, onehot_ref, heads):
    total = jnp.zeros((8, 128), F32)
    for step in range(8):
        rows = [bandg_ref[head * 8 + step : head * 8 + step + 1, :] for head in range(heads)]
        rows.append(jnp.zeros((8 - heads, bandg_ref.shape[1]), F32))
        left = jnp.concatenate(rows, axis=0)
        for _ in range(3):
            low = left.astype(BF16)
            total = total + mm(low, onehot_ref[step], 1, 1)
            left = left - low.astype(F32)
    return total


def gelu_both(inputs):
    half = 0.5 * (1.0 + lax.erf(inputs * HALF_ROOT))
    slope = half + inputs * jnp.exp(-0.5 * inputs * inputs) * BELL_SCALE
    return inputs * half, slope


def chain_kernel(
    dp_count, tensor_count,
    *refs,
):
    count, results = len(INPUTS), 11
    sources, targets, refs = refs[:count], refs[count : count + results], refs[count + results :]
    made, refs = refs[:results], refs[results:]
    held, local_sem, refs = refs[-count - 1 : -1], refs[-1], refs[: -count - 1]
    loads = [
        pltpu.make_async_copy(source, target, local_sem.at[k])
        for k, (source, target) in enumerate(zip(sources, held))
    ]
    for load in loads:
        load.start()
    stores = [
        pltpu.make_async_copy(source, target, local_sem.at[count + k])
        for k, (source, target) in enumerate(zip(made, targets))
    ]
    chain_body(Place(dp_count, tensor_count), loads, stores, *held, *made, *refs)
    for store in stores:
        store.wait()


INPUTS = (
    "layer_input", "output_grad", "segments", "routes", "gate_weights", "onehot", "gain1", "gain2",
    "gain3", "gain4",
    "query1", "key1", "value1", "output1", "bias1", "dense_up", "dense_down",
    "query2", "key2", "value2", "output2", "bias2", "expert_up", "expert_down",
)


def chain_body(
    place, loads, stores,
    x_ref, og_ref, segr_ref, routes_ref, gate_rows, onehot_ref, gain1, gain2, gain3, gain4,
    query1, key1, value1, output1, bias1, dense_up, dense_down, query2, key2, value2, output2,
    bias2, up_ref, down_ref,
    out_ref, xg_ref, arr_ref, arrg_ref, act_ref, gp_ref, sum1_ref, sumd_ref, sum2_ref,
    gain_full, bias_full,
    rows_ref, grows_ref, ogr_ref, part_ref, land_ref, gains_ref, band_ref, bandg_ref,
    w1f_ref, wdf_ref, w2f_ref, qkv_ref, o_ref, pre_ref, x3_ref,
    small_land, small_full, sent_ref, sentg_ref, back_ref, backland_ref, y_ref, yland_ref,
    wg1_ref, wgd_ref, wg2_ref, pair1_ref, paird_ref, pair2_ref,
    gain_grad, gain_land, bias_grad, small_ref, slot_ref, columns_ref, send_sem, recv_sem,
):
    dp_count, tensor_count = place.dp_count, place.tensor_count
    links = Links(send_sem, recv_sem)
    block, features = x_ref.shape
    length = ogr_ref.shape[0]
    heads = band_ref.shape[1] // 8
    top_count = gate_rows.shape[0]
    experts = sent_ref.shape[0]
    slots_one = sent_ref.shape[1] * sent_ref.shape[2]
    own = place.own_rows(block)
    place.greet()
    for load in loads[:-2]:
        load.wait()
    rows_ref[0, own, :] = x_ref[...].astype(BF16)
    ogr_ref[own, :] = og_ref[...].astype(BF16)
    piece = gain1.shape[0]
    own_gains = jnp.concatenate(
        [gain[...].reshape(1, piece) for gain in (gain1, gain2, gain3, gain4)], axis=0
    )
    spot = place_values(piece, (place.dp * tensor_count + place.rank) * piece, features)
    gains = mm(own_gains, spot)
    biases = [
        mm(bias[...], place_values(bias.shape[0], place.dp * bias.shape[0], 128), 0, 0)
        for bias in (bias1, bias2)
    ]
    biases.append(jnp.zeros((heads, features - 256), F32))
    small_ref[...] = jnp.concatenate(
        [gains, jnp.zeros((8 - gains.shape[0], features), F32),
         jnp.concatenate(biases, axis=1), jnp.zeros((8 - heads, features), F32)], axis=0
    ).astype(BF16)
    for full_ref, blocks, last in (
        (w1f_ref, (query1, key1, value1), output1), (w2f_ref, (query2, key2, value2), output2)
    ):
        turned = last[...].astype(F32).T.astype(BF16)
        full_ref[place.dp] = jnp.concatenate([*[ref[...] for ref in blocks], turned], axis=1)
    wdf_ref[place.dp] = jnp.concatenate([dense_up[...], dense_down[...]], axis=1)
    place.met()

    small_land[place.rank] = small_ref[...]
    small_z = [
        links.push(small_ref, small_land.at[place.rank], {"tensor": place.rank_at(offset)})
        for offset in range(1, tensor_count)
    ]
    x_copies = spread_rows(links, place, rows_ref.at[0], block)
    one_started = gather_start(links, place, w1f_ref)
    wait_all(small_z)
    gains = small_land[0, 0:8, :].astype(F32)
    for rank in range(1, tensor_count):
        gains = gains + small_land[rank, 0:8, :].astype(F32)
    small_full[place.dp] = jnp.concatenate(
        [gains, small_ref[8:16, :].astype(F32)], axis=0
    ).astype(BF16)
    small_dp = [
        links.push(small_full.at[place.dp], small_full.at[place.dp], {"dp": place.dp_at(offset)})
        for offset in range(1, dp_count)
    ]
    og_copies = spread_rows(links, place, ogr_ref, block)
    one_passed = gather_forward(links, place, one_started, w1f_ref)
    dense_started = gather_start(links, place, wdf_ref)
    seg_row = segr_ref[...].astype(F32)
    slots = slot_rows(routes_ref, dp_count, experts, sent_ref.shape[2])
    slot_ref[...] = jnp.concatenate(slots, axis=1).astype(jnp.int32)
    lines = [*slots, *[gate_rows[c : c + 1, :] for c in range(top_count)], seg_row]
    lines.append(jnp.zeros((8 - len(lines), length), F32))
    columns_ref[...] = jnp.concatenate(lines, axis=0).T
    allowed = allowed_pairs(seg_row, columns_ref[:, 2 * top_count : 2 * top_count + 1])
    wait_all(small_dp)
    smalls = small_full[0].astype(F32)
    for peer in range(1, dp_count):
        smalls = smalls + small_full[peer].astype(F32)
    gains_ref[...] = smalls[0:8, :]
    make_bands(smalls[8:16, :], onehot_ref, (band_ref.at[0], band_ref.at[1]), heads)
    wait_all(x_copies)
    wait_all(one_passed)

    attn_forward(rows_ref[0], gains_ref[0:1, :], flat(w1f_ref), band_ref.at[0], allowed,
                 qkv_ref.at[0], o_ref.at[0], part_ref.at[0])
    copies = scatter_rows(links, place, part_ref.at[0], land_ref.at[0], block)
    wait_all(og_copies)
    out_rows = ogr_ref[...].astype(F32)
    scaled = jnp.concatenate(
        [(columns_ref[:, top_count + c : top_count + c + 1] * out_rows).astype(BF16) for c in range(top_count)],
        axis=0,
    )
    for e in range(experts):
        chosen = slot_places(slots_one, slot_ref[...] - e * slots_one).astype(BF16)
        sentg_ref[e] = mm(chosen, scaled).astype(BF16).reshape(sentg_ref.shape[1:])
    total, copies = settle(
        links, place, copies, part_ref.at[0], land_ref.at[0], cut(x_ref), rows_ref.at[1]
    )
    dense_passed = gather_forward(links, place, dense_started, wdf_ref)
    two_started = gather_start(links, place, w2f_ref)
    wait_all(copies)
    wait_all(dense_passed)

    hidden = pre_ref.shape[1]
    normed, _, _ = norm_rows(rows_ref[1], gains_ref[1:2, :])
    weights = flat(wdf_ref)
    pre = mm(normed, weights[:, :hidden])
    pre_ref[...] = pre
    part_ref[1] = mm(gelu_value(pre).astype(BF16), weights[:, hidden:], 1, 1).astype(BF16)
    copies = scatter_rows(links, place, part_ref.at[1], land_ref.at[1], block)
    two_passed = gather_forward(links, place, two_started, w2f_ref)
    arrg_copies = [
        swap_start(links, place, sentg_ref, arrg_ref, e) for e in range(experts)
    ]
    total, copies = settle(
        links, place, copies, part_ref.at[1], land_ref.at[1], total, rows_ref.at[2]
    )
    wait_all(copies)
    wait_all(two_passed)

    attn_forward(rows_ref[2], gains_ref[2:3, :], flat(w2f_ref), band_ref.at[1], allowed,
                 qkv_ref.at[1], o_ref.at[1], part_ref.at[2])
    copies = scatter_rows(links, place, part_ref.at[2], land_ref.at[2], block)
    total, copies = settle(
        links, place, copies, part_ref.at[2], land_ref.at[2], total, rows_ref.at[3]
    )
    x3_ref[...] = jnp.concatenate(total, axis=0)
    wait_all(copies)
    normed, _, _ = norm_rows(rows_ref[3], gains_ref[3:4, :])
    arr_copies = []
    for e in range(experts):
        slot_row = slot_ref[...] - e * slots_one
        chosen = slot_places(slots_one, slot_row[:, :length]) | slot_places(
            slots_one, slot_row[:, length:]
        )
        sent_ref[e] = mm(chosen.astype(BF16), normed).astype(BF16).reshape(sent_ref.shape[1:])
        arr_copies.append(swap_start(links, place, sent_ref, arr_ref, e))
    for load in loads[-2:]:
        load.wait()

    back_copies, y_copies = [], []
    for e in range(experts):
        wait_all(arrg_copies[e])
        grad_active = mm(flat(arrg_ref.at[e]), down_ref[e], 1, 1)
        wait_all(arr_copies[e])
        active, slope = gelu_both(mm(flat(arr_ref.at[e]), up_ref[e]))
        act_ref[e] = active.astype(BF16)
        gp_ref[e] = (grad_active * slope).astype(BF16)
        back_ref[e] = mm(gp_ref[e], up_ref[e], 1, 1).astype(BF16).reshape(back_ref.shape[1:])
        back_copies.append(swap_start(links, place, back_ref, backland_ref, e))
    for e in range(experts):
        y_ref[e] = mm(act_ref[e], down_ref[e]).astype(BF16).reshape(y_ref.shape[1:])
        y_copies.append(swap_start(links, place, y_ref, yland_ref, e))

    for store in stores[2:6]:
        store.start()
    lanes = lax.broadcasted_iota(jnp.int32, (length, slots_one), 1)
    normed, normal, inv_rms = norm_rows(rows_ref[3], gains_ref[3:4, :])
    grad_normed = jnp.zeros((length, features), F32)
    for e in range(experts):
        slot_cols = columns_ref[:, 0:top_count].astype(jnp.int32) - e * slots_one
        chosen = (lanes == slot_cols[:, 0:1]) | (lanes == slot_cols[:, 1:2])
        wait_all(back_copies[e])
        grad_normed = grad_normed + mm(chosen.astype(BF16), flat(backland_ref.at[e]))
    grad_part, gain_grad[3:4, :] = norm_back(grad_normed, normal, inv_rms, gains_ref[3:4, :])
    part_ref[3] = grad_part.astype(BF16)
    copies = scatter_rows(links, place, part_ref.at[3], land_ref.at[3], block)
    total, copies = settle(
        links, place, copies, part_ref.at[3], land_ref.at[3], cut(og_ref), grows_ref.at[0]
    )
    wait_all(copies)

    kept = attn_backward(
        grows_ref[0], rows_ref[2], gains_ref[2:3, :], flat(w2f_ref), band_ref.at[1], allowed,
        qkv_ref.at[1], o_ref.at[1], part_ref.at[4], gain_grad.at[2:3, :], bandg_ref.at[1],
    )
    copies = scatter_rows(links, place, part_ref.at[4], land_ref.at[4], block)
    attn_weights_grad(grows_ref[0], kept, wg2_ref)
    two_sum = sum_start(links, place, wg2_ref, pair2_ref)
    total, copies = settle(
        links, place, copies, part_ref.at[4], land_ref.at[4], total, grows_ref.at[1]
    )
    two_copies = sum_onward(links, place, two_sum, wg2_ref, pair2_ref, sum2_ref)
    combined = jnp.zeros((length, features), F32)
    for e in range(experts):
        wait_all(y_copies[e])
        returned = flat(yland_ref.at[e])
        slot_cols = columns_ref[:, 0:top_count].astype(jnp.int32) - e * slots_one
        for c in range(top_count):
            chosen = (lanes == slot_cols[:, c : c + 1]).astype(BF16)
            combined = combined + columns_ref[:, top_count + c : top_count + c + 1] * mm(chosen, returned)
    part_ref[5] = combined.astype(BF16)
    wait_all(copies)
    out_copies = scatter_rows(links, place, part_ref.at[5], land_ref.at[5], block)

    normed, normal, inv_rms = norm_rows(rows_ref[1], gains_ref[1:2, :])
    grad_rows = grows_ref[1]
    weights = flat(wdf_ref)
    active, slope = gelu_both(pre_ref[...])
    grad_pre = (mm(grad_rows, weights[:, hidden:]) * slope).astype(BF16)
    grad_normed = mm(grad_pre, weights[:, :hidden], 1, 1)
    grad_part, gain_grad[1:2, :] = norm_back(grad_normed, normal, inv_rms, gains_ref[1:2, :])
    part_ref[6] = grad_part.astype(BF16)
    copies = scatter_rows(links, place, part_ref.at[6], land_ref.at[6], block)
    wgd_ref[:, :, :, :hidden] = mm(normed, grad_pre, 0, 0).astype(BF16).reshape(
        *wgd_ref.shape[:3], hidden
    )
    wgd_ref[:, :, :, hidden:] = mm(grad_rows, active.astype(BF16), 0, 0).astype(BF16).reshape(
        *wgd_ref.shape[:3], hidden
    )
    dense_sum = sum_start(links, place, wgd_ref, paird_ref)
    total, copies = settle(
        links, place, copies, part_ref.at[6], land_ref.at[6], total, grows_ref.at[2]
    )
    dense_copies = sum_onward(links, place, dense_sum, wgd_ref, paird_ref, sumd_ref)
    sums, _ = settle(links, place, out_copies, part_ref.at[5], land_ref.at[5], cut(x3_ref))
    out_ref[...] = jnp.concatenate(sums, axis=0)
    stores[0].start()
    bias_two = bias_sums(bandg_ref.at[1], onehot_ref, heads)
    wait_all(copies)

    kept = attn_backward(
        grows_ref[2], rows_ref[0], gains_ref[0:1, :], flat(w1f_ref), band_ref.at[0], allowed,
        qkv_ref.at[0], o_ref.at[0], part_ref.at[7], gain_grad.at[0:1, :], bandg_ref.at[0],
    )
    gain_grad[4:8, :] = jnp.zeros((4, features), F32)
    gain_z = [
        links.push(gain_grad, gain_land.at[offset - 1], {"tensor": place.rank_at(offset)})
        for offset in range(1, tensor_count)
    ]
    copies = scatter_rows(links, place, part_ref.at[7], land_ref.at[7], block)
    attn_weights_grad(grows_ref[2], kept, wg1_ref)
    one_sum = sum_start(links, place, wg1_ref, pair1_ref)
    bias_grad[...] = jnp.concatenate(
        [bias_sums(bandg_ref.at[0], onehot_ref, heads), bias_two], axis=1
    )
    bias_full[place.dp] = bias_grad[...]
    last = [
        links.push(bias_grad, bias_full.at[place.dp], {"dp": place.dp_at(offset)})
        for offset in range(1, dp_count)
    ]
    one_copies = sum_onward(links, place, one_sum, wg1_ref, pair1_ref, sum1_ref)
    gains = gain_grad[...]
    for offset, copy in enumerate(gain_z):
        copy.wait_recv()
        gains = gains + gain_land[offset]
    gain_full[place.dp] = gains
    last += [
        links.push(gain_full.at[place.dp], gain_full.at[place.dp], {"dp": place.dp_at(offset)})
        for offset in range(1, dp_count)
    ]
    total, _ = settle(links, place, copies, part_ref.at[7], land_ref.at[7], total)
    xg_ref[...] = jnp.concatenate(total, axis=0)
    stores[1].start()
    wait_all(two_copies)
    stores[8].start()
    wait_all(dense_copies)
    stores[7].start()
    wait_all(one_copies)
    stores[6].start()
    wait_all(last)
    stores[9].start()
    stores[10].start()
    links.finish()


def finish_kernel(
    *refs,
):
    sources, refs = refs[:11], refs[11:]
    held, load_sem, refs = refs[-12:-1], refs[-1], refs[:-12]
    loads = [
        pltpu.make_async_copy(source, target, load_sem.at[k])
        for k, (source, target) in enumerate(zip(sources, held))
    ]
    for k in (9, 10, 4, 6, 5, 7, 8, 1, 2, 0, 3):
        loads[k].start()
    arr_ref, arrg_ref, act_ref, gp_ref, sum1_ref, sumd_ref, sum2_ref, gain_full, bias_full = held[:9]
    layer_ref, grad_ref = held[9:]
    layer_out, grad_out, *refs = refs
    gain_outs, bias_outs = refs[:4], refs[4:6]
    refs = refs[6:]
    outs, (upg_out, downg_out) = refs[:10], refs[10:12]
    stages, (upg_ref, downg_ref), sem = refs[12:22], refs[22:24], refs[24]
    experts = act_ref.shape[0]
    copies = []

    def send(source, target):
        copy = pltpu.make_async_copy(source, target, sem.at[len(copies)])
        copy.start()
        copies.append(copy)

    for k in (9, 10, 4, 6, 5, 7, 8):
        loads[k].wait()
    send(layer_ref, layer_out)
    send(grad_ref, grad_out)

    def added(ref):
        total = ref[0].astype(F32)
        for k in range(1, ref.shape[0]):
            total = total + ref[k].astype(F32)
        return total

    one, two, dense = added(sum1_ref), added(sum2_ref), added(sumd_ref)
    width, hidden = one.shape[1] // 4, dense.shape[1] // 2
    values = []
    for total in (one, two):
        values += [total[:, k * width : (k + 1) * width] for k in range(3)]
        values.append(total[:, 3 * width :].T)
    values += [dense[:, :hidden], dense[:, hidden:]]
    for value, stage, out in zip(values, stages, outs):
        stage[...] = value
        send(stage, out)
    for k in (1, 2):
        loads[k].wait()
    for e in range(experts):
        downg_ref[e] = mm(act_ref[e], flat(arrg_ref.at[e]), 0, 0)
        send(downg_ref.at[e], downg_out.at[e])
    for k in (0, 3):
        loads[k].wait()
    for e in range(experts):
        upg_ref[e] = mm(flat(arr_ref.at[e]), gp_ref[e], 0, 0)
        send(upg_ref.at[e], upg_out.at[e])
    piece = gain_outs[0].shape[0]
    me = lax.axis_index("dp")
    start = (me * lax.axis_size("tensor") + lax.axis_index("tensor")) * piece
    gains = added(gain_full)
    features = gains.shape[1]
    gains = pltpu.roll(gains, lax.rem(features - start, features), 1)
    for k, out in enumerate(gain_outs):
        out[...] = gains[k, :piece]
    biases = added(bias_full)
    count, heads = bias_outs[0].shape
    for layer, out in enumerate(bias_outs):
        block = biases[:, layer * 128 : layer * 128 + 128]
        block = pltpu.roll(block, lax.rem(128 - me * count, 128), 1)
        out[...] = block.T[:count, :heads]
    for copy in copies:
        copy.wait()


def on_device(
    layer_input, segments, routes, gate_weights,
    first_gain, first_query, first_key, first_value, first_output, first_bias,
    first_dense_gain, first_dense_up, first_dense_down,
    second_gain, second_query, second_key, second_value, second_output, second_bias,
    second_expert_gain, expert_up, expert_down, output_grad,
):
    dp_count, tensor_count = lax.axis_size("dp"), lax.axis_size("tensor")
    length = segments.shape[1]
    features = layer_input.shape[1]
    width = first_query.shape[1]
    heads = first_bias.shape[1]
    hidden = first_dense_up.shape[1]
    top_count = routes.shape[1]
    local_experts = expert_up.shape[0]
    expert_count = local_experts * dp_count
    capacity = max(2, 3 * length * top_count // (2 * expert_count))
    capacity = -(-capacity // 16) * 16
    swap_shape = (local_experts, dp_count, capacity, features)
    slots_one = dp_count * capacity
    weight_rows = first_query.shape[0]
    block = layer_input.shape[0]
    wide = 4 * width
    groups = dp_count // 2
    outs = [
        ((block, features), F32), ((block, features), F32), (swap_shape, BF16), (swap_shape, BF16),
        ((local_experts, slots_one, hidden), BF16), ((local_experts, slots_one, hidden), BF16),
        ((groups, weight_rows, wide), BF16), ((groups, weight_rows, 2 * hidden), BF16),
        ((groups, weight_rows, wide), BF16),
        ((dp_count, 8, features), F32), ((dp_count, 8, 256), F32),
    ]
    full = lambda columns: pltpu.VMEM((dp_count, weight_rows, columns), BF16)
    split = lambda columns: pltpu.VMEM((groups, 2, weight_rows, columns), BF16)
    half = lambda columns: pltpu.VMEM((groups, weight_rows, columns), BF16)
    columns = (wide, 2 * hidden, wide)
    copies = 14 * PIECES * tensor_count + 12 * tensor_count + 18 * dp_count
    inputs = (
        layer_input, output_grad, segments, routes.T, gate_weights.T,
        jnp.asarray(band_steps(length, BUCKETS), BF16),
        first_gain, first_dense_gain, second_gain, second_expert_gain,
        first_query, first_key, first_value, first_output, first_bias,
        first_dense_up, first_dense_down.T,
        second_query, second_key, second_value, second_output, second_bias,
        expert_up, expert_down,
    )
    scratch = [
        *[pltpu.VMEM(shape, dtype) for shape, dtype in outs],
        pltpu.VMEM((4, length, features), BF16),
        pltpu.VMEM((3, length, features), BF16),
        pltpu.VMEM((length, features), BF16),
        pltpu.VMEM((8, length, features), BF16),
        pltpu.VMEM((8, tensor_count - 1, block, features), BF16),
        pltpu.VMEM((8, features), F32),
        pltpu.VMEM((2, heads * 8, length), F32),
        pltpu.VMEM((2, heads * 8, length), F32),
        *[full(n) for n in columns],
        pltpu.VMEM((2, length, 3 * width), BF16),
        pltpu.VMEM((2, length, width), BF16),
        pltpu.VMEM((length, hidden), F32),
        pltpu.VMEM((block, features), F32),
        pltpu.VMEM((tensor_count, 16, features), BF16),
        pltpu.VMEM((dp_count, 16, features), BF16),
        *[pltpu.VMEM(swap_shape, BF16)] * 6,
        *[split(n) for n in columns],
        *[half(n) for n in columns],
        pltpu.VMEM((8, features), F32),
        pltpu.VMEM((tensor_count - 1, 8, features), F32),
        pltpu.VMEM((8, 256), F32),
        pltpu.VMEM((16, features), BF16),
        pltpu.VMEM((1, top_count * length), jnp.int32),
        pltpu.VMEM((length, 8), F32),
        pltpu.SemaphoreType.DMA((copies,)),
        pltpu.SemaphoreType.DMA((copies,)),
        *[pltpu.VMEM(one.shape, one.dtype) for one in inputs],
        pltpu.SemaphoreType.DMA((len(inputs) + len(outs),)),
    ]
    vmem = pl.BlockSpec(memory_space=pltpu.VMEM)
    anywhere = pl.BlockSpec(memory_space=pl.ANY)
    made = pl.pallas_call(
        functools.partial(chain_kernel, dp_count, tensor_count),
        out_shape=[jax.ShapeDtypeStruct(shape, dtype) for shape, dtype in outs],
        in_specs=[anywhere] * len(inputs),
        out_specs=[anywhere] * len(outs),
        scratch_shapes=scratch,
        compiler_params=pltpu.CompilerParams(
            collective_id=1, has_side_effects=True, vmem_limit_bytes=60 * 1024 * 1024
        ),
    )(*inputs)
    layer_sum, grad_sum, *kept = made
    four = [(weight_rows, width)] * 3 + [(width, weight_rows)]
    pieces = four + four + [(weight_rows, hidden), (weight_rows, hidden)]
    shapes = [(block, features), (block, features), *[first_gain.shape] * 4,
              *[first_bias.shape] * 2, *pieces, expert_up.shape, expert_down.shape]
    finished = pl.pallas_call(
        finish_kernel,
        out_shape=[jax.ShapeDtypeStruct(shape, F32) for shape in shapes],
        in_specs=[anywhere] * 11,
        out_specs=[anywhere] * 2 + [vmem] * 6 + [anywhere] * 12,
        scratch_shapes=[
            *[pltpu.VMEM(shape, F32) for shape in pieces],
            pltpu.VMEM(expert_up.shape, F32),
            pltpu.VMEM(expert_down.shape, F32),
            pltpu.SemaphoreType.DMA((12 + 2 * local_experts,)),
            *[pltpu.VMEM(shape, dtype) for shape, dtype in outs[2:] + outs[:2]],
            pltpu.SemaphoreType.DMA((11,)),
        ],
        compiler_params=pltpu.CompilerParams(vmem_limit_bytes=60 * 1024 * 1024),
    )(*kept, layer_sum, grad_sum)
    layer_output, input_grad, *grads = finished
    gains, biases, grads = grads[:4], grads[4:6], grads[6:]
    return (
        layer_output, input_grad,
        gains[0], *grads[0:4], biases[0],
        gains[1], grads[8], grads[9].T,
        gains[2], *grads[4:8], biases[1],
        gains[3], *grads[10:],
    )


def solution(mesh):
    attn = (P("dp", "tensor"), P("dp", "tensor"), P("dp", "tensor"), P("tensor", "dp"),
            P("dp", "tensor"))
    both = P(("dp", "tensor"))
    rows = P(("dp", "tensor"), None)
    return jax.shard_map(
        on_device,
        mesh=mesh,
        in_specs=(
            rows, P("dp", None), P("dp", None), P("dp", None),
            both, *attn,
            both, P("dp", "tensor"), P("tensor", "dp"),
            both, *attn,
            both, P("dp", None, "tensor"), P("dp", "tensor", None), rows,
        ),
        out_specs=(
            rows, rows,
            both, *attn,
            both, P("dp", "tensor"), P("tensor", "dp"),
            both, *attn,
            both, P("dp", None, "tensor"), P("dp", "tensor", None),
        ),
        check_vma=False,
    )
```

```python
import functools
import math

import jax
import jax.numpy as jnp
import numpy as np
from jax import lax
from jax.experimental import pallas as pl
from jax.experimental.pallas import tpu as pltpu
from jax.sharding import PartitionSpec as P

DH = 64
BUCKETS = 32
EPSILON = 1e-06
NEG_FILL = -1e30
HALF_ROOT = 0.7071067811865476
BELL_SCALE = 0.3989422804014327
F32 = jnp.float32
BF16 = jnp.bfloat16
PIECES = 2


def band_onehot(length, buckets):
    exact_count = buckets // 2
    distance = np.arange(length)
    result = np.minimum(distance, exact_count)
    for bucket_level in range(1, exact_count):
        threshold = int(
            np.ceil(exact_count * (128.0 / exact_count) ** (bucket_level / exact_count))
        )
        result = result + (distance >= threshold)
    band = result[(np.arange(8)[:, None] - np.arange(length)[None, :]) % length]
    return (band.reshape(-1)[:, None] == np.arange(buckets)[None, :]).astype(np.float32)


def band_steps(length, buckets):
    table = band_onehot(length, buckets).reshape(8, length, buckets).transpose(0, 2, 1)
    return np.pad(table, ((0, 0), (0, 128 - buckets), (0, 0)))


def gelu_value(inputs):
    return 0.5 * inputs * (1.0 + lax.erf(inputs * HALF_ROOT))


def gelu_slope(inputs):
    return (
        0.5 * (1.0 + lax.erf(inputs * HALF_ROOT))
        + inputs * jnp.exp(-0.5 * inputs * inputs) * BELL_SCALE
    )


def norm_rows(token_rows, gain_full):
    values = token_rows.astype(F32)
    inv_rms = lax.rsqrt(jnp.mean(values * values, axis=-1, keepdims=True) + EPSILON)
    normal = values * inv_rms
    return ((normal * gain_full).astype(BF16), normal, inv_rms)


def norm_back(grad_normed, normal, inv_rms, gain_full):
    grad_normal = grad_normed * gain_full
    grad_part = inv_rms * (
        grad_normal - normal * jnp.mean(grad_normal * normal, axis=-1, keepdims=True)
    )
    return (grad_part, jnp.sum(grad_normed * normal, axis=0, keepdims=True))


def mm(left, right, left_dim=1, right_dim=0):
    return lax.dot_general(
        left, right, (((left_dim,), (right_dim,)), ((), ())), preferred_element_type=F32
    )


def allowed_pairs(seg_row, seg_col):
    length = seg_row.shape[1]
    rows = lax.broadcasted_iota(jnp.int32, (length, length), 0)
    cols = lax.broadcasted_iota(jnp.int32, (length, length), 1)
    return (rows >= cols) & (seg_row == seg_col)


def head_shares(query, key, band, allowed):
    length = query.shape[0]
    bias = jnp.concatenate(
        [pltpu.roll(band, 8 * step, 1) if step else band for step in range(length // 8)], axis=0
    )
    scores = mm(query, key, 1, 1) * (1.0 / math.sqrt(DH)) + bias
    scores = jnp.where(allowed, scores, NEG_FILL)
    exp_scores = jnp.exp(scores - jnp.max(scores, axis=-1, keepdims=True))
    return exp_scores / jnp.sum(exp_scores, axis=-1, keepdims=True)


MESH = pl.DeviceIdType.MESH


class Links:
    def __init__(self, send_sem, recv_sem):
        self.send_sem, self.recv_sem = send_sem, recv_sem
        self.copies = []

    def push(self, source, target, where):
        index = len(self.copies)
        copy = pltpu.make_async_remote_copy(
            src_ref=source, dst_ref=target, send_sem=self.send_sem.at[index],
            recv_sem=self.recv_sem.at[index], device_id=where, device_id_type=MESH,
        )
        copy.start()
        self.copies.append(copy)
        return copy

    def finish(self):
        for copy in self.copies:
            copy.wait_send()


class Place:
    def __init__(self, dp_count, tensor_count):
        self.dp_count, self.tensor_count = dp_count, tensor_count
        self.groups = dp_count // 2
        self.dp = lax.axis_index("dp")
        self.rank = lax.axis_index("tensor")
        self.side = lax.rem(self.dp, 2)
        self.group = lax.div(self.dp, 2)
        self.twin = {"dp": self.dp + 1 - 2 * self.side}

    def rank_at(self, offset):
        return lax.rem(self.rank + offset, self.tensor_count)

    def group_at(self, offset):
        return lax.rem(self.group + offset, self.groups)

    def dp_at(self, offset):
        return lax.rem(self.dp + offset, self.dp_count)

    def greet(self):
        barrier = pltpu.get_barrier_semaphore()
        partners = [{"tensor": self.rank_at(o)} for o in range(1, self.tensor_count)]
        partners += [{"dp": self.dp_at(o)} for o in range(1, self.dp_count)]
        for partner in partners:
            pl.semaphore_signal(barrier, inc=1, device_id=partner, device_id_type=MESH)

    def met(self):
        pl.semaphore_wait(
            pltpu.get_barrier_semaphore(), self.tensor_count + self.dp_count - 2
        )

    def own_rows(self, block):
        return pl.ds(pl.multiple_of(self.rank * block, block), block)


def wait_all(copies):
    for copy in copies:
        copy.wait_recv()


def spread_rows(links, place, rows_ref, block):
    own = place.own_rows(block)
    return [
        links.push(rows_ref.at[own, :], rows_ref.at[own, :], {"tensor": place.rank_at(offset)})
        for offset in range(1, place.tensor_count)
    ]


def piece_rows(start, block, piece):
    size = block // PIECES
    return pl.ds(pl.multiple_of(start + piece * size, size), size)


def scatter_rows(links, place, part_ref, land_ref, block, which=range(PIECES)):
    pieces = []
    for piece in which:
        copies = []
        for offset in range(1, place.tensor_count):
            peer = place.rank_at(offset)
            copies.append(
                links.push(
                    part_ref.at[piece_rows(peer * block, block, piece), :],
                    land_ref.at[offset - 1, piece_rows(0, block, piece)], {"tensor": peer},
                )
            )
        pieces.append(copies)
    return pieces


def settle(links, place, pieces, part_ref, land_ref, resid, rows_ref=None):
    block = land_ref.shape[1]
    totals, spread = [], []
    for piece, copies in enumerate(pieces):
        own = piece_rows(place.rank * block, block, piece)
        total = part_ref[own, :].astype(F32)
        for offset, copy in enumerate(copies):
            copy.wait_recv()
            total = total + land_ref[offset, piece_rows(0, block, piece)].astype(F32)
        total = resid[piece] + total
        totals.append(total)
        if rows_ref is not None:
            rows_ref[own, :] = total.astype(BF16)
            for offset in range(1, place.tensor_count):
                spread.append(
                    links.push(
                        rows_ref.at[own, :], rows_ref.at[own, :],
                        {"tensor": place.rank_at(offset)},
                    )
                )
    return totals, spread


def cut(ref):
    block = ref.shape[0]
    return [ref[piece_rows(0, block, piece), :] for piece in range(PIECES)]


def gather_start(links, place, full_ref):
    first = links.push(full_ref.at[place.dp], full_ref.at[place.dp], place.twin)
    others = [
        links.push(
            full_ref.at[place.dp], full_ref.at[place.dp],
            {"dp": place.group_at(offset) * 2 + place.side},
        )
        for offset in range(1, place.groups)
    ]
    return first, others


def gather_forward(links, place, started, full_ref):
    first, others = started
    passed = [first]
    for offset, copy in enumerate(others, 1):
        copy.wait_recv()
        origin = place.group_at(place.groups - offset) * 2 + place.side
        passed.append(links.push(full_ref.at[origin], full_ref.at[origin], place.twin))
    return passed


def swap_start(links, place, sent_ref, arrived_ref, part):
    copies = []
    for offset in range(1, place.dp_count):
        peer = place.dp_at(offset)
        copies.append(
            links.push(sent_ref.at[part, peer], arrived_ref.at[part, place.dp], {"dp": peer})
        )
    arrived_ref[part, place.dp] = sent_ref[part, place.dp]
    return copies


def flat(ref):
    count, rows, columns = ref.shape
    return ref[...].reshape(count * rows, columns)


def attn_forward(x_rows, gain, weights, band_ref, allowed, qkv_ref, o_ref, part_ref, shares_ref):
    normed, _, _ = norm_rows(x_rows, gain)
    width = o_ref.shape[1]
    qkv = mm(normed, weights[:, : 3 * width]).astype(BF16)
    qkv_ref[...] = qkv
    mixed = []
    for head in range(width // DH):
        lo = head * DH
        shares = head_shares(
            qkv[:, lo : lo + DH],
            qkv[:, width + lo : width + lo + DH],
            band_ref[head * 8 : head * 8 + 8, :],
            allowed,
        )
        shares_ref[head] = shares
        mixed.append(mm(shares.astype(BF16), qkv[:, 2 * width + lo : 2 * width + lo + DH]).astype(BF16))
    mixed = jnp.concatenate(mixed, axis=1)
    o_ref[...] = mixed
    part_ref[...] = mm(mixed, weights[:, 3 * width :], 1, 1).astype(BF16)


def slot_places(slots, slot_row):
    shape = (slots, slot_row.shape[1])
    return lax.broadcasted_iota(jnp.int32, shape, 0) == slot_row


def slot_rows(routes_ref, dp_count, experts, capacity):
    top_count, length = routes_ref.shape
    named = []
    for c in range(top_count):
        row = routes_ref[c : c + 1, :]
        first = lax.broadcasted_iota(jnp.int32, (dp_count, length), 0) * experts
        named.append(
            jnp.concatenate(
                [jnp.where(first + e == row, 1.0, 0.0) for e in range(experts)], axis=0
            )
        )
    total = named[0]
    for one in named[1:]:
        total = total + one
    shape = (length, length)
    earlier = lax.broadcasted_iota(jnp.int32, shape, 0) < lax.broadcasted_iota(jnp.int32, shape, 1)
    before = mm(total.astype(BF16), jnp.where(earlier, 1.0, 0.0).astype(BF16))
    start = lax.broadcasted_iota(jnp.int32, before.shape, 0).astype(F32) * capacity
    return [jnp.sum(one * (start + before), axis=0, keepdims=True) for one in named]


def place_values(count, start, columns):
    shape = (count, columns)
    rows = lax.broadcasted_iota(jnp.int32, shape, 0)
    target = rows + start == lax.broadcasted_iota(jnp.int32, shape, 1)
    return jnp.where(target, 1.0, 0.0).astype(BF16)


def make_bands(biases, onehot_ref, band_refs, heads):
    length = onehot_ref.shape[2]
    for layer, band_ref in enumerate(band_refs):
        block = biases[:, layer * 128 : layer * 128 + 128].astype(BF16)
        rows = [mm(block, onehot_ref[step]) for step in range(8)]
        for head in range(heads):
            band_ref[head * 8 : head * 8 + 8, :] = jnp.concatenate(
                [row[head : head + 1, :] for row in rows], axis=0
            )


def attn_backward(grad_rows, normed_rows, gain, weights, shares_ref, qkv_ref, o_ref,
                  part_ref, gain_ref, score_ref):
    width = o_ref.shape[1]
    normed, normal, inv_rms = normed_rows
    mixed = o_ref[...]
    qkv = qkv_ref[...]
    grad_mixed = mm(grad_rows, weights[:, 3 * width :]).astype(BF16)
    inv_root = 1.0 / math.sqrt(DH)
    grad_q, grad_k, grad_v = [], [], []
    for head in range(width // DH):
        lo = head * DH
        query = qkv[:, lo : lo + DH]
        key = qkv[:, width + lo : width + lo + DH]
        value = qkv[:, 2 * width + lo : 2 * width + lo + DH]
        grad_head = grad_mixed[:, lo : lo + DH]
        mixed_head = mixed[:, lo : lo + DH]
        shares = shares_ref[head]
        grad_v.append(mm(shares.astype(BF16), grad_head, 0, 0).astype(BF16))
        row_dot = jnp.sum(
            grad_head.astype(F32) * mixed_head.astype(F32), axis=-1, keepdims=True
        )
        score_grad = shares * (mm(grad_head, value, 1, 1) - row_dot)
        score_ref[head] = score_grad
        score_low = score_grad.astype(BF16)
        grad_q.append((mm(score_low, key) * inv_root).astype(BF16))
        grad_k.append((mm(score_low, query, 0, 0) * inv_root).astype(BF16))
    grad_qkv = jnp.concatenate(grad_q + grad_k + grad_v, axis=1)
    grad_normed = mm(grad_qkv, weights[:, : 3 * width], 1, 1)
    grad_part, gain_grad = norm_back(grad_normed, normal, inv_rms, gain)
    part_ref[...] = grad_part.astype(BF16)
    gain_ref[...] = gain_grad
    return normed, grad_qkv, mixed


def band_sums(score_ref, bandg_ref):
    heads, length = score_ref.shape[:2]
    for head in range(heads):
        total = score_ref[head, 0:8, :]
        for step in range(1, length // 8):
            total = total + pltpu.roll(
                score_ref[head, 8 * step : 8 * step + 8, :], length - 8 * step, 1
            )
        bandg_ref[head * 8 : head * 8 + 8, :] = total


def attn_weights_grad(grad_rows, kept, wg_ref):
    normed, grad_qkv, mixed = kept
    wg = jnp.concatenate(
        [mm(normed, grad_qkv, 0, 0).astype(BF16), mm(grad_rows, mixed, 0, 0).astype(BF16)], axis=1
    )
    wg_ref[...] = wg.reshape(wg_ref.shape)


def sum_start(links, place, wg_ref, pair_ref):
    return links.push(wg_ref.at[:, 1 - place.side], pair_ref, place.twin)


def sum_onward(links, place, started, wg_ref, pair_ref, out_ref):
    started.wait_recv()
    pair_ref[...] = (
        wg_ref[:, place.side].astype(F32) + pair_ref[...].astype(F32)
    ).astype(BF16)
    copies = []
    for offset in range(1, place.groups):
        peer = place.group_at(offset)
        copies.append(
            links.push(pair_ref.at[peer], out_ref.at[offset], {"dp": peer * 2 + place.side})
        )
    out_ref[0] = pair_ref[place.group]
    return copies


def bias_sums(bandg_ref, onehot_ref, heads):
    total = jnp.zeros((8, 128), F32)
    for step in range(8):
        rows = [bandg_ref[head * 8 + step : head * 8 + step + 1, :] for head in range(heads)]
        rows.append(jnp.zeros((8 - heads, bandg_ref.shape[1]), F32))
        left = jnp.concatenate(rows, axis=0)
        for _ in range(3):
            low = left.astype(BF16)
            total = total + mm(low, onehot_ref[step], 1, 1)
            left = left - low.astype(F32)
    return total


def gelu_both(inputs):
    half = 0.5 * (1.0 + lax.erf(inputs * HALF_ROOT))
    slope = half + inputs * jnp.exp(-0.5 * inputs * inputs) * BELL_SCALE
    return inputs * half, slope


def chain_kernel(
    dp_count, tensor_count,
    *refs,
):
    count, results = len(INPUTS), 11
    sources, targets, refs = refs[:count], refs[count : count + results], refs[count + results :]
    made, refs = refs[:results], refs[results:]
    held, local_sem, refs = refs[-count - 1 : -1], refs[-1], refs[: -count - 1]
    loads = [
        pltpu.make_async_copy(source, target, local_sem.at[k])
        for k, (source, target) in enumerate(zip(sources, held))
    ]
    for load in loads[:-2]:
        load.start()
    stores = [
        pltpu.make_async_copy(source, target, local_sem.at[count + k])
        for k, (source, target) in enumerate(zip(made, targets))
    ]
    chain_body(Place(dp_count, tensor_count), loads, stores, *held, *made, *refs)
    for store in stores:
        store.wait()


INPUTS = (
    "layer_input", "output_grad", "segments", "routes", "gate_weights", "onehot", "gain1", "gain2",
    "gain3", "gain4",
    "query1", "key1", "value1", "output1", "bias1", "dense_up", "dense_down",
    "query2", "key2", "value2", "output2", "bias2", "expert_up", "expert_down",
)


def chain_body(
    place, loads, stores,
    x_ref, og_ref, segr_ref, routes_ref, gate_rows, onehot_ref, gain1, gain2, gain3, gain4,
    query1, key1, value1, output1, bias1, dense_up, dense_down, query2, key2, value2, output2,
    bias2, up_ref, down_ref,
    out_ref, xg_ref, arr_ref, arrg_ref, act_ref, gp_ref, sum1_ref, sumd_ref, sum2_ref,
    gain_full, bias_full,
    rows_ref, grows_ref, ogr_ref, part_ref, land_ref, gains_ref, band_ref, bandg_ref,
    w1f_ref, wdf_ref, w2f_ref, qkv_ref, o_ref, pre_ref, x3_ref,
    small_land, small_full, sent_ref, sentg_ref, back_ref, backland_ref, y_ref, yland_ref,
    wg1_ref, wgd_ref, wg2_ref, pair1_ref, paird_ref, pair2_ref,
    gain_grad, gain_land, bias_grad, small_ref, slot_ref, columns_ref, shares_ref, score_ref,
    active_ref, send_sem, recv_sem,
):
    dp_count, tensor_count = place.dp_count, place.tensor_count
    links = Links(send_sem, recv_sem)
    block, features = x_ref.shape
    length = ogr_ref.shape[0]
    heads = band_ref.shape[1] // 8
    top_count = gate_rows.shape[0]
    experts = sent_ref.shape[0]
    slots_one = sent_ref.shape[1] * sent_ref.shape[2]
    own = place.own_rows(block)
    place.greet()
    for load in loads[:-2]:
        load.wait()
    rows_ref[0, own, :] = x_ref[...].astype(BF16)
    ogr_ref[own, :] = og_ref[...].astype(BF16)
    piece = gain1.shape[0]
    own_gains = jnp.concatenate(
        [gain[...].reshape(1, piece) for gain in (gain1, gain2, gain3, gain4)], axis=0
    )
    spot = place_values(piece, (place.dp * tensor_count + place.rank) * piece, features)
    gains = mm(own_gains, spot)
    biases = [
        mm(bias[...], place_values(bias.shape[0], place.dp * bias.shape[0], 128), 0, 0)
        for bias in (bias1, bias2)
    ]
    biases.append(jnp.zeros((heads, features - 256), F32))
    small_ref[...] = jnp.concatenate(
        [gains, jnp.zeros((8 - gains.shape[0], features), F32),
         jnp.concatenate(biases, axis=1), jnp.zeros((8 - heads, features), F32)], axis=0
    ).astype(BF16)
    for full_ref, blocks, last in (
        (w1f_ref, (query1, key1, value1), output1), (w2f_ref, (query2, key2, value2), output2)
    ):
        turned = last[...].astype(F32).T.astype(BF16)
        full_ref[place.dp] = jnp.concatenate([*[ref[...] for ref in blocks], turned], axis=1)
    wdf_ref[place.dp] = jnp.concatenate([dense_up[...], dense_down[...]], axis=1)
    place.met()

    small_land[place.rank] = small_ref[...]
    small_z = [
        links.push(small_ref, small_land.at[place.rank], {"tensor": place.rank_at(offset)})
        for offset in range(1, tensor_count)
    ]
    x_copies = spread_rows(links, place, rows_ref.at[0], block)
    one_started = gather_start(links, place, w1f_ref)
    for load in loads[-2:]:
        load.start()
    wait_all(small_z)
    gains = small_land[0, 0:8, :].astype(F32)
    for rank in range(1, tensor_count):
        gains = gains + small_land[rank, 0:8, :].astype(F32)
    small_full[place.dp] = jnp.concatenate(
        [gains, small_ref[8:16, :].astype(F32)], axis=0
    ).astype(BF16)
    small_dp = [
        links.push(small_full.at[place.dp], small_full.at[place.dp], {"dp": place.dp_at(offset)})
        for offset in range(1, dp_count)
    ]
    og_copies = spread_rows(links, place, ogr_ref, block)
    one_passed = gather_forward(links, place, one_started, w1f_ref)
    dense_started = gather_start(links, place, wdf_ref)
    seg_row = segr_ref[...].astype(F32)
    slots = slot_rows(routes_ref, dp_count, experts, sent_ref.shape[2])
    slot_ref[...] = jnp.concatenate(slots, axis=1).astype(jnp.int32)
    lines = [*slots, *[gate_rows[c : c + 1, :] for c in range(top_count)], seg_row]
    lines.append(jnp.zeros((8 - len(lines), length), F32))
    columns_ref[...] = jnp.concatenate(lines, axis=0).T
    allowed = allowed_pairs(seg_row, columns_ref[:, 2 * top_count : 2 * top_count + 1])
    wait_all(small_dp)
    smalls = small_full[0].astype(F32)
    for peer in range(1, dp_count):
        smalls = smalls + small_full[peer].astype(F32)
    gains_ref[...] = smalls[0:8, :]
    make_bands(smalls[8:16, :], onehot_ref, (band_ref.at[0], band_ref.at[1]), heads)
    wait_all(x_copies)
    wait_all(one_passed)

    attn_forward(rows_ref[0], gains_ref[0:1, :], flat(w1f_ref), band_ref.at[0], allowed,
                 qkv_ref.at[0], o_ref.at[0], part_ref.at[0], shares_ref.at[0])
    copies = scatter_rows(links, place, part_ref.at[0], land_ref.at[0], block)
    wait_all(og_copies)
    out_rows = ogr_ref[...].astype(F32)
    scaled = jnp.concatenate(
        [(columns_ref[:, top_count + c : top_count + c + 1] * out_rows).astype(BF16) for c in range(top_count)],
        axis=0,
    )
    for e in range(experts):
        chosen = slot_places(slots_one, slot_ref[...] - e * slots_one).astype(BF16)
        sentg_ref[e] = mm(chosen, scaled).astype(BF16).reshape(sentg_ref.shape[1:])
    total, copies = settle(
        links, place, copies, part_ref.at[0], land_ref.at[0], cut(x_ref), rows_ref.at[1]
    )
    dense_passed = gather_forward(links, place, dense_started, wdf_ref)
    two_started = gather_start(links, place, w2f_ref)
    wait_all(copies)
    wait_all(dense_passed)

    hidden = pre_ref.shape[1]
    normed, _, _ = norm_rows(rows_ref[1], gains_ref[1:2, :])
    weights = flat(wdf_ref)
    pre = mm(normed, weights[:, :hidden])
    pre_ref[...] = pre
    active_ref[...] = gelu_value(pre).astype(BF16)
    part_ref[1] = mm(active_ref[...], weights[:, hidden:], 1, 1).astype(BF16)
    copies = scatter_rows(links, place, part_ref.at[1], land_ref.at[1], block)
    two_passed = gather_forward(links, place, two_started, w2f_ref)
    pre_ref[...] = gelu_slope(pre_ref[...])
    arrg_copies = [
        swap_start(links, place, sentg_ref, arrg_ref, e) for e in range(experts)
    ]
    total, copies = settle(
        links, place, copies, part_ref.at[1], land_ref.at[1], total, rows_ref.at[2]
    )
    wait_all(copies)
    wait_all(two_passed)

    attn_forward(rows_ref[2], gains_ref[2:3, :], flat(w2f_ref), band_ref.at[1], allowed,
                 qkv_ref.at[1], o_ref.at[1], part_ref.at[2], shares_ref.at[1])
    copies = scatter_rows(links, place, part_ref.at[2], land_ref.at[2], block)
    total, copies = settle(
        links, place, copies, part_ref.at[2], land_ref.at[2], total, rows_ref.at[3]
    )
    x3_ref[...] = jnp.concatenate(total, axis=0)
    wait_all(copies)
    normed, _, _ = norm_rows(rows_ref[3], gains_ref[3:4, :])
    arr_copies = []
    for e in range(experts):
        slot_row = slot_ref[...] - e * slots_one
        chosen = slot_places(slots_one, slot_row[:, :length]) | slot_places(
            slots_one, slot_row[:, length:]
        )
        sent_ref[e] = mm(chosen.astype(BF16), normed).astype(BF16).reshape(sent_ref.shape[1:])
        arr_copies.append(swap_start(links, place, sent_ref, arr_ref, e))
    for load in loads[-2:]:
        load.wait()

    back_copies, y_copies = [], []
    for e in range(experts):
        wait_all(arrg_copies[e])
        grad_active = mm(flat(arrg_ref.at[e]), down_ref[e], 1, 1)
        wait_all(arr_copies[e])
        active, slope = gelu_both(mm(flat(arr_ref.at[e]), up_ref[e]))
        act_ref[e] = active.astype(BF16)
        gp_ref[e] = (grad_active * slope).astype(BF16)
        back_ref[e] = mm(gp_ref[e], up_ref[e], 1, 1).astype(BF16).reshape(back_ref.shape[1:])
        back_copies.append(swap_start(links, place, back_ref, backland_ref, e))
    for e in range(experts):
        y_ref[e] = mm(act_ref[e], down_ref[e]).astype(BF16).reshape(y_ref.shape[1:])
        y_copies.append(swap_start(links, place, y_ref, yland_ref, e))

    for store in stores[2:6]:
        store.start()
    lanes = lax.broadcasted_iota(jnp.int32, (length, slots_one), 1)
    normed, normal, inv_rms = norm_rows(rows_ref[3], gains_ref[3:4, :])
    grad_normed = jnp.zeros((length, features), F32)
    for e in range(experts):
        slot_cols = columns_ref[:, 0:top_count].astype(jnp.int32) - e * slots_one
        chosen = (lanes == slot_cols[:, 0:1]) | (lanes == slot_cols[:, 1:2])
        wait_all(back_copies[e])
        grad_normed = grad_normed + mm(chosen.astype(BF16), flat(backland_ref.at[e]))
    grad_part, gain_grad[3:4, :] = norm_back(grad_normed, normal, inv_rms, gains_ref[3:4, :])
    part_ref[3] = grad_part.astype(BF16)
    copies = scatter_rows(links, place, part_ref.at[3], land_ref.at[3], block)
    total, copies = settle(
        links, place, copies, part_ref.at[3], land_ref.at[3], cut(og_ref), grows_ref.at[0]
    )
    normed_rows = norm_rows(rows_ref[2], gains_ref[2:3, :])
    wait_all(copies)

    kept = attn_backward(
        grows_ref[0], normed_rows, gains_ref[2:3, :], flat(w2f_ref), shares_ref.at[1],
        qkv_ref.at[1], o_ref.at[1], part_ref.at[4], gain_grad.at[2:3, :], score_ref,
    )
    copies = scatter_rows(links, place, part_ref.at[4], land_ref.at[4], block)
    attn_weights_grad(grows_ref[0], kept, wg2_ref)
    two_sum = sum_start(links, place, wg2_ref, pair2_ref)
    band_sums(score_ref, bandg_ref.at[1])
    total, copies = settle(
        links, place, copies, part_ref.at[4], land_ref.at[4], total, grows_ref.at[1]
    )
    two_copies = sum_onward(links, place, two_sum, wg2_ref, pair2_ref, sum2_ref)
    combined = jnp.zeros((length, features), F32)
    for e in range(experts):
        wait_all(y_copies[e])
        returned = flat(yland_ref.at[e])
        slot_cols = columns_ref[:, 0:top_count].astype(jnp.int32) - e * slots_one
        for c in range(top_count):
            chosen = (lanes == slot_cols[:, c : c + 1]).astype(BF16)
            combined = combined + columns_ref[:, top_count + c : top_count + c + 1] * mm(chosen, returned)
    part_ref[5] = combined.astype(BF16)
    normed, normal, inv_rms = norm_rows(rows_ref[1], gains_ref[1:2, :])
    wait_all(copies)
    out_copies = scatter_rows(
        links, place, part_ref.at[5], land_ref.at[5], block, range(PIECES // 2)
    )

    grad_rows = grows_ref[1]
    weights = flat(wdf_ref)
    grad_pre = (mm(grad_rows, weights[:, hidden:]) * pre_ref[...]).astype(BF16)
    grad_normed = mm(grad_pre, weights[:, :hidden], 1, 1)
    grad_part, gain_grad[1:2, :] = norm_back(grad_normed, normal, inv_rms, gains_ref[1:2, :])
    part_ref[6] = grad_part.astype(BF16)
    copies = scatter_rows(links, place, part_ref.at[6], land_ref.at[6], block)
    wgd_ref[:, :, :, :hidden] = mm(normed, grad_pre, 0, 0).astype(BF16).reshape(
        *wgd_ref.shape[:3], hidden
    )
    wgd_ref[:, :, :, hidden:] = mm(grad_rows, active_ref[...], 0, 0).astype(BF16).reshape(
        *wgd_ref.shape[:3], hidden
    )
    dense_sum = sum_start(links, place, wgd_ref, paird_ref)
    total, copies = settle(
        links, place, copies, part_ref.at[6], land_ref.at[6], total, grows_ref.at[2]
    )
    dense_copies = sum_onward(links, place, dense_sum, wgd_ref, paird_ref, sumd_ref)
    bias_two = bias_sums(bandg_ref.at[1], onehot_ref, heads)
    normed_rows = norm_rows(rows_ref[0], gains_ref[0:1, :])
    wait_all(copies)
    out_copies += scatter_rows(
        links, place, part_ref.at[5], land_ref.at[5], block, range(PIECES // 2, PIECES)
    )

    kept = attn_backward(
        grows_ref[2], normed_rows, gains_ref[0:1, :], flat(w1f_ref), shares_ref.at[0],
        qkv_ref.at[0], o_ref.at[0], part_ref.at[7], gain_grad.at[0:1, :], score_ref,
    )
    gain_grad[4:8, :] = jnp.zeros((4, features), F32)
    gain_z = [
        links.push(gain_grad, gain_land.at[offset - 1], {"tensor": place.rank_at(offset)})
        for offset in range(1, tensor_count)
    ]
    copies = scatter_rows(links, place, part_ref.at[7], land_ref.at[7], block)
    attn_weights_grad(grows_ref[2], kept, wg1_ref)
    one_sum = sum_start(links, place, wg1_ref, pair1_ref)
    band_sums(score_ref, bandg_ref.at[0])
    bias_grad[...] = jnp.concatenate(
        [bias_sums(bandg_ref.at[0], onehot_ref, heads), bias_two], axis=1
    )
    bias_full[place.dp] = bias_grad[...]
    last = [
        links.push(bias_grad, bias_full.at[place.dp], {"dp": place.dp_at(offset)})
        for offset in range(1, dp_count)
    ]
    sums, _ = settle(links, place, out_copies, part_ref.at[5], land_ref.at[5], cut(x3_ref))
    out_ref[...] = jnp.concatenate(sums, axis=0)
    stores[0].start()
    one_copies = sum_onward(links, place, one_sum, wg1_ref, pair1_ref, sum1_ref)
    gains = gain_grad[...]
    for offset, copy in enumerate(gain_z):
        copy.wait_recv()
        gains = gains + gain_land[offset]
    gain_full[place.dp] = gains
    last += [
        links.push(gain_full.at[place.dp], gain_full.at[place.dp], {"dp": place.dp_at(offset)})
        for offset in range(1, dp_count)
    ]
    total, _ = settle(links, place, copies, part_ref.at[7], land_ref.at[7], total)
    xg_ref[...] = jnp.concatenate(total, axis=0)
    stores[1].start()
    wait_all(two_copies)
    stores[8].start()
    wait_all(dense_copies)
    stores[7].start()
    wait_all(one_copies)
    stores[6].start()
    wait_all(last)
    stores[9].start()
    stores[10].start()
    links.finish()


def finish_kernel(
    *refs,
):
    sources, refs = refs[:11], refs[11:]
    held, load_sem, refs = refs[-12:-1], refs[-1], refs[:-12]
    loads = [
        pltpu.make_async_copy(source, target, load_sem.at[k])
        for k, (source, target) in enumerate(zip(sources, held))
    ]
    for k in (9, 10, 4, 6, 5, 7, 8, 1, 2, 0, 3):
        loads[k].start()
    arr_ref, arrg_ref, act_ref, gp_ref, sum1_ref, sumd_ref, sum2_ref, gain_full, bias_full = held[:9]
    layer_ref, grad_ref = held[9:]
    layer_out, grad_out, *refs = refs
    gain_outs, bias_outs = refs[:4], refs[4:6]
    refs = refs[6:]
    outs, (upg_out, downg_out) = refs[:10], refs[10:12]
    stages, (upg_ref, downg_ref), sem = refs[12:22], refs[22:24], refs[24]
    experts = act_ref.shape[0]
    copies = []

    def send(source, target):
        copy = pltpu.make_async_copy(source, target, sem.at[len(copies)])
        copy.start()
        copies.append(copy)

    for k in (9, 10, 4, 6, 5, 7, 8):
        loads[k].wait()
    send(layer_ref, layer_out)
    send(grad_ref, grad_out)

    def added(ref):
        total = ref[0].astype(F32)
        for k in range(1, ref.shape[0]):
            total = total + ref[k].astype(F32)
        return total

    one, two, dense = added(sum1_ref), added(sum2_ref), added(sumd_ref)
    width, hidden = one.shape[1] // 4, dense.shape[1] // 2
    values = []
    for total in (one, two):
        values += [total[:, k * width : (k + 1) * width] for k in range(3)]
        values.append(total[:, 3 * width :].T)
    values += [dense[:, :hidden], dense[:, hidden:]]
    for value, stage, out in zip(values, stages, outs):
        stage[...] = value
        send(stage, out)
    for k in (1, 2):
        loads[k].wait()
    for e in range(experts):
        downg_ref[e] = mm(act_ref[e], flat(arrg_ref.at[e]), 0, 0)
        send(downg_ref.at[e], downg_out.at[e])
    for k in (0, 3):
        loads[k].wait()
    for e in range(experts):
        upg_ref[e] = mm(flat(arr_ref.at[e]), gp_ref[e], 0, 0)
        send(upg_ref.at[e], upg_out.at[e])
    piece = gain_outs[0].shape[0]
    me = lax.axis_index("dp")
    start = (me * lax.axis_size("tensor") + lax.axis_index("tensor")) * piece
    gains = added(gain_full)
    features = gains.shape[1]
    gains = pltpu.roll(gains, lax.rem(features - start, features), 1)
    for k, out in enumerate(gain_outs):
        out[...] = gains[k, :piece]
    biases = added(bias_full)
    count, heads = bias_outs[0].shape
    for layer, out in enumerate(bias_outs):
        block = biases[:, layer * 128 : layer * 128 + 128]
        block = pltpu.roll(block, lax.rem(128 - me * count, 128), 1)
        out[...] = block.T[:count, :heads]
    for copy in copies:
        copy.wait()


def on_device(
    layer_input, segments, routes, gate_weights,
    first_gain, first_query, first_key, first_value, first_output, first_bias,
    first_dense_gain, first_dense_up, first_dense_down,
    second_gain, second_query, second_key, second_value, second_output, second_bias,
    second_expert_gain, expert_up, expert_down, output_grad,
):
    dp_count, tensor_count = lax.axis_size("dp"), lax.axis_size("tensor")
    length = segments.shape[1]
    features = layer_input.shape[1]
    width = first_query.shape[1]
    heads = first_bias.shape[1]
    hidden = first_dense_up.shape[1]
    top_count = routes.shape[1]
    local_experts = expert_up.shape[0]
    expert_count = local_experts * dp_count
    capacity = max(2, 3 * length * top_count // (2 * expert_count))
    capacity = -(-capacity // 16) * 16
    swap_shape = (local_experts, dp_count, capacity, features)
    slots_one = dp_count * capacity
    weight_rows = first_query.shape[0]
    block = layer_input.shape[0]
    wide = 4 * width
    groups = dp_count // 2
    outs = [
        ((block, features), F32), ((block, features), F32), (swap_shape, BF16), (swap_shape, BF16),
        ((local_experts, slots_one, hidden), BF16), ((local_experts, slots_one, hidden), BF16),
        ((groups, weight_rows, wide), BF16), ((groups, weight_rows, 2 * hidden), BF16),
        ((groups, weight_rows, wide), BF16),
        ((dp_count, 8, features), F32), ((dp_count, 8, 256), F32),
    ]
    full = lambda columns: pltpu.VMEM((dp_count, weight_rows, columns), BF16)
    split = lambda columns: pltpu.VMEM((groups, 2, weight_rows, columns), BF16)
    half = lambda columns: pltpu.VMEM((groups, weight_rows, columns), BF16)
    columns = (wide, 2 * hidden, wide)
    copies = 14 * PIECES * tensor_count + 12 * tensor_count + 18 * dp_count
    inputs = (
        layer_input, output_grad, segments, routes.T, gate_weights.T,
        jnp.asarray(band_steps(length, BUCKETS), BF16),
        first_gain, first_dense_gain, second_gain, second_expert_gain,
        first_query, first_key, first_value, first_output, first_bias,
        first_dense_up, first_dense_down.T,
        second_query, second_key, second_value, second_output, second_bias,
        expert_up, expert_down,
    )
    scratch = [
        *[pltpu.VMEM(shape, dtype) for shape, dtype in outs],
        pltpu.VMEM((4, length, features), BF16),
        pltpu.VMEM((3, length, features), BF16),
        pltpu.VMEM((length, features), BF16),
        pltpu.VMEM((8, length, features), BF16),
        pltpu.VMEM((8, tensor_count - 1, block, features), BF16),
        pltpu.VMEM((8, features), F32),
        pltpu.VMEM((2, heads * 8, length), F32),
        pltpu.VMEM((2, heads * 8, length), F32),
        *[full(n) for n in columns],
        pltpu.VMEM((2, length, 3 * width), BF16),
        pltpu.VMEM((2, length, width), BF16),
        pltpu.VMEM((length, hidden), F32),
        pltpu.VMEM((block, features), F32),
        pltpu.VMEM((tensor_count, 16, features), BF16),
        pltpu.VMEM((dp_count, 16, features), BF16),
        *[pltpu.VMEM(swap_shape, BF16)] * 6,
        *[split(n) for n in columns],
        *[half(n) for n in columns],
        pltpu.VMEM((8, features), F32),
        pltpu.VMEM((tensor_count - 1, 8, features), F32),
        pltpu.VMEM((8, 256), F32),
        pltpu.VMEM((16, features), BF16),
        pltpu.VMEM((1, top_count * length), jnp.int32),
        pltpu.VMEM((length, 8), F32),
        pltpu.VMEM((2, heads, length, length), F32),
        pltpu.VMEM((heads, length, length), F32),
        pltpu.VMEM((length, hidden), BF16),
        pltpu.SemaphoreType.DMA((copies,)),
        pltpu.SemaphoreType.DMA((copies,)),
        *[pltpu.VMEM(one.shape, one.dtype) for one in inputs],
        pltpu.SemaphoreType.DMA((len(inputs) + len(outs),)),
    ]
    vmem = pl.BlockSpec(memory_space=pltpu.VMEM)
    anywhere = pl.BlockSpec(memory_space=pl.ANY)
    made = pl.pallas_call(
        functools.partial(chain_kernel, dp_count, tensor_count),
        out_shape=[jax.ShapeDtypeStruct(shape, dtype) for shape, dtype in outs],
        in_specs=[anywhere] * len(inputs),
        out_specs=[anywhere] * len(outs),
        scratch_shapes=scratch,
        compiler_params=pltpu.CompilerParams(
            collective_id=1, has_side_effects=True, vmem_limit_bytes=60 * 1024 * 1024
        ),
    )(*inputs)
    layer_sum, grad_sum, *kept = made
    four = [(weight_rows, width)] * 3 + [(width, weight_rows)]
    pieces = four + four + [(weight_rows, hidden), (weight_rows, hidden)]
    shapes = [(block, features), (block, features), *[first_gain.shape] * 4,
              *[first_bias.shape] * 2, *pieces, expert_up.shape, expert_down.shape]
    finished = pl.pallas_call(
        finish_kernel,
        out_shape=[jax.ShapeDtypeStruct(shape, F32) for shape in shapes],
        in_specs=[anywhere] * 11,
        out_specs=[anywhere] * 2 + [vmem] * 6 + [anywhere] * 12,
        scratch_shapes=[
            *[pltpu.VMEM(shape, F32) for shape in pieces],
            pltpu.VMEM(expert_up.shape, F32),
            pltpu.VMEM(expert_down.shape, F32),
            pltpu.SemaphoreType.DMA((12 + 2 * local_experts,)),
            *[pltpu.VMEM(shape, dtype) for shape, dtype in outs[2:] + outs[:2]],
            pltpu.SemaphoreType.DMA((11,)),
        ],
        compiler_params=pltpu.CompilerParams(vmem_limit_bytes=60 * 1024 * 1024),
    )(*kept, layer_sum, grad_sum)
    layer_output, input_grad, *grads = finished
    gains, biases, grads = grads[:4], grads[4:6], grads[6:]
    return (
        layer_output, input_grad,
        gains[0], *grads[0:4], biases[0],
        gains[1], grads[8], grads[9].T,
        gains[2], *grads[4:8], biases[1],
        gains[3], *grads[10:],
    )


def solution(mesh):
    attn = (P("dp", "tensor"), P("dp", "tensor"), P("dp", "tensor"), P("tensor", "dp"),
            P("dp", "tensor"))
    both = P(("dp", "tensor"))
    rows = P(("dp", "tensor"), None)
    return jax.shard_map(
        on_device,
        mesh=mesh,
        in_specs=(
            rows, P("dp", None), P("dp", None), P("dp", None),
            both, *attn,
            both, P("dp", "tensor"), P("tensor", "dp"),
            both, *attn,
            both, P("dp", None, "tensor"), P("dp", "tensor", None), rows,
        ),
        out_specs=(
            rows, rows,
            both, *attn,
            both, P("dp", "tensor"), P("tensor", "dp"),
            both, *attn,
            both, P("dp", None, "tensor"), P("dp", "tensor", None),
        ),
        check_vma=False,
    )
```

```python
import functools
import math

import jax
import jax.numpy as jnp
import numpy as np
from jax import lax
from jax.experimental import pallas as pl
from jax.experimental.pallas import tpu as pltpu
from jax.sharding import PartitionSpec as P

DH = 64
BUCKETS = 32
EPSILON = 1e-06
NEG_FILL = -1e30
HALF_ROOT = 0.7071067811865476
BELL_SCALE = 0.3989422804014327
F32 = jnp.float32
BF16 = jnp.bfloat16
PIECES = 2


def band_onehot(length, buckets):
    exact_count = buckets // 2
    distance = np.arange(length)
    result = np.minimum(distance, exact_count)
    for bucket_level in range(1, exact_count):
        threshold = int(
            np.ceil(exact_count * (128.0 / exact_count) ** (bucket_level / exact_count))
        )
        result = result + (distance >= threshold)
    band = result[(np.arange(8)[:, None] - np.arange(length)[None, :]) % length]
    return (band.reshape(-1)[:, None] == np.arange(buckets)[None, :]).astype(np.float32)


def band_steps(length, buckets):
    table = band_onehot(length, buckets).reshape(8, length, buckets).transpose(0, 2, 1)
    return np.pad(table, ((0, 0), (0, 128 - buckets), (0, 0)))


def gelu_value(inputs):
    return 0.5 * inputs * (1.0 + lax.erf(inputs * HALF_ROOT))


def gelu_slope(inputs):
    return (
        0.5 * (1.0 + lax.erf(inputs * HALF_ROOT))
        + inputs * jnp.exp(-0.5 * inputs * inputs) * BELL_SCALE
    )


def norm_rows(token_rows, gain_full):
    values = token_rows.astype(F32)
    inv_rms = lax.rsqrt(jnp.mean(values * values, axis=-1, keepdims=True) + EPSILON)
    normal = values * inv_rms
    return ((normal * gain_full).astype(BF16), normal, inv_rms)


def norm_back(grad_normed, normal, inv_rms, gain_full):
    grad_normal = grad_normed * gain_full
    grad_part = inv_rms * (
        grad_normal - normal * jnp.mean(grad_normal * normal, axis=-1, keepdims=True)
    )
    return (grad_part, jnp.sum(grad_normed * normal, axis=0, keepdims=True))


def mm(left, right, left_dim=1, right_dim=0):
    return lax.dot_general(
        left, right, (((left_dim,), (right_dim,)), ((), ())), preferred_element_type=F32
    )


def allowed_pairs(seg_row, seg_col):
    length = seg_row.shape[1]
    rows = lax.broadcasted_iota(jnp.int32, (length, length), 0)
    cols = lax.broadcasted_iota(jnp.int32, (length, length), 1)
    return (rows >= cols) & (seg_row == seg_col)


def head_shares(query, key, band, allowed):
    length = query.shape[0]
    bias = jnp.concatenate(
        [pltpu.roll(band, 8 * step, 1) if step else band for step in range(length // 8)], axis=0
    )
    scores = mm(query, key, 1, 1) * (1.0 / math.sqrt(DH)) + bias
    scores = jnp.where(allowed, scores, NEG_FILL)
    exp_scores = jnp.exp(scores - jnp.max(scores, axis=-1, keepdims=True))
    return exp_scores / jnp.sum(exp_scores, axis=-1, keepdims=True)


MESH = pl.DeviceIdType.MESH


class Links:
    def __init__(self, send_sem, recv_sem):
        self.send_sem, self.recv_sem = send_sem, recv_sem
        self.copies = []

    def push(self, source, target, where):
        index = len(self.copies)
        copy = pltpu.make_async_remote_copy(
            src_ref=source, dst_ref=target, send_sem=self.send_sem.at[index],
            recv_sem=self.recv_sem.at[index], device_id=where, device_id_type=MESH,
        )
        copy.start()
        self.copies.append(copy)
        return copy

    def finish(self):
        for copy in self.copies:
            copy.wait_send()


class Place:
    def __init__(self, dp_count, tensor_count):
        self.dp_count, self.tensor_count = dp_count, tensor_count
        self.groups = dp_count // 2
        self.dp = lax.axis_index("dp")
        self.rank = lax.axis_index("tensor")
        self.side = lax.rem(self.dp, 2)
        self.group = lax.div(self.dp, 2)
        self.twin = {"dp": self.dp + 1 - 2 * self.side}

    def rank_at(self, offset):
        return lax.rem(self.rank + offset, self.tensor_count)

    def group_at(self, offset):
        return lax.rem(self.group + offset, self.groups)

    def dp_at(self, offset):
        return lax.rem(self.dp + offset, self.dp_count)

    def greet(self):
        barrier = pltpu.get_barrier_semaphore()
        partners = [{"tensor": self.rank_at(o)} for o in range(1, self.tensor_count)]
        partners += [{"dp": self.dp_at(o)} for o in range(1, self.dp_count)]
        for partner in partners:
            pl.semaphore_signal(barrier, inc=1, device_id=partner, device_id_type=MESH)

    def met(self):
        pl.semaphore_wait(
            pltpu.get_barrier_semaphore(), self.tensor_count + self.dp_count - 2
        )

    def own_rows(self, block):
        return pl.ds(pl.multiple_of(self.rank * block, block), block)


def wait_all(copies):
    for copy in copies:
        copy.wait_recv()


def spread_rows(links, place, rows_ref, block):
    own = place.own_rows(block)
    return [
        links.push(rows_ref.at[own, :], rows_ref.at[own, :], {"tensor": place.rank_at(offset)})
        for offset in range(1, place.tensor_count)
    ]


def piece_rows(start, block, piece):
    size = block // PIECES
    return pl.ds(pl.multiple_of(start + piece * size, size), size)


def scatter_rows(links, place, part_ref, land_ref, block, which=range(PIECES)):
    pieces = []
    for piece in which:
        copies = []
        for offset in range(1, place.tensor_count):
            peer = place.rank_at(offset)
            copies.append(
                links.push(
                    part_ref.at[piece_rows(peer * block, block, piece), :],
                    land_ref.at[offset - 1, piece_rows(0, block, piece)], {"tensor": peer},
                )
            )
        pieces.append(copies)
    return pieces


def settle(links, place, pieces, part_ref, land_ref, resid, rows_ref=None):
    block = land_ref.shape[1]
    totals, spread = [], []
    for piece, copies in enumerate(pieces):
        own = piece_rows(place.rank * block, block, piece)
        total = part_ref[own, :].astype(F32)
        for offset, copy in enumerate(copies):
            copy.wait_recv()
            total = total + land_ref[offset, piece_rows(0, block, piece)].astype(F32)
        total = resid[piece] + total
        totals.append(total)
        if rows_ref is not None:
            rows_ref[own, :] = total.astype(BF16)
            for offset in range(1, place.tensor_count):
                spread.append(
                    links.push(
                        rows_ref.at[own, :], rows_ref.at[own, :],
                        {"tensor": place.rank_at(offset)},
                    )
                )
    return totals, spread


def cut(ref):
    block = ref.shape[0]
    return [ref[piece_rows(0, block, piece), :] for piece in range(PIECES)]


def gather_start(links, place, full_ref):
    first = links.push(full_ref.at[place.dp], full_ref.at[place.dp], place.twin)
    others = [
        links.push(
            full_ref.at[place.dp], full_ref.at[place.dp],
            {"dp": place.group_at(offset) * 2 + place.side},
        )
        for offset in range(1, place.groups)
    ]
    return first, others


def gather_forward(links, place, started, full_ref):
    first, others = started
    passed = [first]
    for offset, copy in enumerate(others, 1):
        copy.wait_recv()
        origin = place.group_at(place.groups - offset) * 2 + place.side
        passed.append(links.push(full_ref.at[origin], full_ref.at[origin], place.twin))
    return passed


def swap_start(links, place, sent_ref, arrived_ref, part):
    copies = []
    for offset in range(1, place.dp_count):
        peer = place.dp_at(offset)
        copies.append(
            links.push(sent_ref.at[part, peer], arrived_ref.at[part, place.dp], {"dp": peer})
        )
    arrived_ref[part, place.dp] = sent_ref[part, place.dp]
    return copies


def flat(ref):
    count, rows, columns = ref.shape
    return ref[...].reshape(count * rows, columns)


def attn_forward(x_rows, gain, weights, band_ref, allowed, qkv_ref, o_ref, part_ref, shares_ref):
    normed, _, _ = norm_rows(x_rows, gain)
    width = o_ref.shape[1]
    qkv = mm(normed, weights[:, : 3 * width]).astype(BF16)
    qkv_ref[...] = qkv
    mixed = []
    for head in range(width // DH):
        lo = head * DH
        shares = head_shares(
            qkv[:, lo : lo + DH],
            qkv[:, width + lo : width + lo + DH],
            band_ref[head * 8 : head * 8 + 8, :],
            allowed,
        )
        shares_ref[head] = shares
        mixed.append(mm(shares.astype(BF16), qkv[:, 2 * width + lo : 2 * width + lo + DH]).astype(BF16))
    mixed = jnp.concatenate(mixed, axis=1)
    o_ref[...] = mixed
    part_ref[...] = mm(mixed, weights[:, 3 * width :], 1, 1).astype(BF16)


def slot_places(slots, slot_row):
    shape = (slots, slot_row.shape[1])
    return lax.broadcasted_iota(jnp.int32, shape, 0) == slot_row


def slot_rows(routes_ref, dp_count, experts, capacity):
    top_count, length = routes_ref.shape
    named = []
    for c in range(top_count):
        row = routes_ref[c : c + 1, :]
        first = lax.broadcasted_iota(jnp.int32, (dp_count, length), 0) * experts
        named.append(
            jnp.concatenate(
                [jnp.where(first + e == row, 1.0, 0.0) for e in range(experts)], axis=0
            )
        )
    total = named[0]
    for one in named[1:]:
        total = total + one
    shape = (length, length)
    earlier = lax.broadcasted_iota(jnp.int32, shape, 0) < lax.broadcasted_iota(jnp.int32, shape, 1)
    before = mm(total.astype(BF16), jnp.where(earlier, 1.0, 0.0).astype(BF16))
    start = lax.broadcasted_iota(jnp.int32, before.shape, 0).astype(F32) * capacity
    return [jnp.sum(one * (start + before), axis=0, keepdims=True) for one in named]


def place_values(count, start, columns):
    shape = (count, columns)
    rows = lax.broadcasted_iota(jnp.int32, shape, 0)
    target = rows + start == lax.broadcasted_iota(jnp.int32, shape, 1)
    return jnp.where(target, 1.0, 0.0).astype(BF16)


def make_bands(biases, onehot_ref, band_refs, heads):
    length = onehot_ref.shape[2]
    for layer, band_ref in enumerate(band_refs):
        block = biases[:, layer * 128 : layer * 128 + 128].astype(BF16)
        rows = [mm(block, onehot_ref[step]) for step in range(8)]
        for head in range(heads):
            band_ref[head * 8 : head * 8 + 8, :] = jnp.concatenate(
                [row[head : head + 1, :] for row in rows], axis=0
            )


def attn_backward(grad_rows, normed_rows, gain, weights, shares_ref, qkv_ref, o_ref,
                  part_ref, gain_ref, score_ref):
    width = o_ref.shape[1]
    normed, normal, inv_rms = normed_rows
    mixed = o_ref[...]
    qkv = qkv_ref[...]
    grad_mixed = mm(grad_rows, weights[:, 3 * width :]).astype(BF16)
    inv_root = 1.0 / math.sqrt(DH)
    grad_q, grad_k, grad_v = [], [], []
    for head in range(width // DH):
        lo = head * DH
        query = qkv[:, lo : lo + DH]
        key = qkv[:, width + lo : width + lo + DH]
        value = qkv[:, 2 * width + lo : 2 * width + lo + DH]
        grad_head = grad_mixed[:, lo : lo + DH]
        mixed_head = mixed[:, lo : lo + DH]
        shares = shares_ref[head]
        grad_v.append(mm(shares.astype(BF16), grad_head, 0, 0).astype(BF16))
        row_dot = jnp.sum(
            grad_head.astype(F32) * mixed_head.astype(F32), axis=-1, keepdims=True
        )
        score_grad = shares * (mm(grad_head, value, 1, 1) - row_dot)
        score_ref[head] = score_grad
        score_low = score_grad.astype(BF16)
        grad_q.append((mm(score_low, key) * inv_root).astype(BF16))
        grad_k.append((mm(score_low, query, 0, 0) * inv_root).astype(BF16))
    grad_qkv = jnp.concatenate(grad_q + grad_k + grad_v, axis=1)
    grad_normed = mm(grad_qkv, weights[:, : 3 * width], 1, 1)
    grad_part, gain_grad = norm_back(grad_normed, normal, inv_rms, gain)
    part_ref[...] = grad_part.astype(BF16)
    gain_ref[...] = gain_grad
    return normed, grad_qkv, mixed


def band_sums(score_ref, bandg_ref):
    heads, length = score_ref.shape[:2]
    for head in range(heads):
        total = score_ref[head, 0:8, :]
        for step in range(1, length // 8):
            total = total + pltpu.roll(
                score_ref[head, 8 * step : 8 * step + 8, :], length - 8 * step, 1
            )
        bandg_ref[head * 8 : head * 8 + 8, :] = total


def attn_weights_grad(grad_rows, kept, wg_ref):
    normed, grad_qkv, mixed = kept
    wg = jnp.concatenate(
        [mm(normed, grad_qkv, 0, 0).astype(BF16), mm(grad_rows, mixed, 0, 0).astype(BF16)], axis=1
    )
    wg_ref[...] = wg.reshape(wg_ref.shape)


def sum_start(links, place, wg_ref, pair_ref):
    return links.push(wg_ref.at[:, 1 - place.side], pair_ref, place.twin)


def sum_onward(links, place, started, wg_ref, pair_ref, out_ref):
    started.wait_recv()
    pair_ref[...] = (
        wg_ref[:, place.side].astype(F32) + pair_ref[...].astype(F32)
    ).astype(BF16)
    copies = []
    for offset in range(1, place.groups):
        peer = place.group_at(offset)
        copies.append(
            links.push(pair_ref.at[peer], out_ref.at[offset], {"dp": peer * 2 + place.side})
        )
    out_ref[0] = pair_ref[place.group]
    return copies


def bias_sums(bandg_ref, onehot_ref, heads):
    total = jnp.zeros((8, 128), F32)
    for step in range(8):
        rows = [bandg_ref[head * 8 + step : head * 8 + step + 1, :] for head in range(heads)]
        rows.append(jnp.zeros((8 - heads, bandg_ref.shape[1]), F32))
        left = jnp.concatenate(rows, axis=0)
        for _ in range(3):
            low = left.astype(BF16)
            total = total + mm(low, onehot_ref[step], 1, 1)
            left = left - low.astype(F32)
    return total


def gelu_both(inputs):
    half = 0.5 * (1.0 + lax.erf(inputs * HALF_ROOT))
    slope = half + inputs * jnp.exp(-0.5 * inputs * inputs) * BELL_SCALE
    return inputs * half, slope


def chain_kernel(
    dp_count, tensor_count,
    *refs,
):
    count, results = len(INPUTS), 11
    sources, targets, refs = refs[:count], refs[count : count + results], refs[count + results :]
    made, refs = refs[:results], refs[results:]
    held, local_sem, refs = refs[-count - 1 : -1], refs[-1], refs[: -count - 1]
    loads = [
        pltpu.make_async_copy(source, target, local_sem.at[k])
        for k, (source, target) in enumerate(zip(sources, held))
    ]
    for load in loads[:-2]:
        load.start()
    stores = [
        pltpu.make_async_copy(source, target, local_sem.at[count + k])
        for k, (source, target) in enumerate(zip(made, targets))
    ]
    chain_body(Place(dp_count, tensor_count), loads, stores, *held, *made, *refs)
    for store in stores:
        store.wait()


INPUTS = (
    "layer_input", "output_grad", "segments", "routes", "gate_weights", "onehot", "gain1", "gain2",
    "gain3", "gain4",
    "query1", "key1", "value1", "output1", "bias1", "dense_up", "dense_down",
    "query2", "key2", "value2", "output2", "bias2", "expert_up", "expert_down",
)


def chain_body(
    place, loads, stores,
    x_ref, og_ref, segr_ref, routes_ref, gate_rows, onehot_ref, gain1, gain2, gain3, gain4,
    query1, key1, value1, output1, bias1, dense_up, dense_down, query2, key2, value2, output2,
    bias2, up_ref, down_ref,
    out_ref, xg_ref, arr_ref, arrg_ref, act_ref, gp_ref, sum1_ref, sumd_ref, sum2_ref,
    gain_full, bias_full,
    rows_ref, grows_ref, ogr_ref, part_ref, land_ref, gains_ref, band_ref, bandg_ref,
    w1f_ref, wdf_ref, w2f_ref, qkv_ref, o_ref, pre_ref, x3_ref,
    small_land, small_full, sent_ref, sentg_ref, back_ref, backland_ref, y_ref, yland_ref,
    wg1_ref, wgd_ref, wg2_ref, pair1_ref, paird_ref, pair2_ref,
    gain_grad, gain_land, bias_grad, small_ref, slot_ref, columns_ref, shares_ref, score_ref,
    active_ref, send_sem, recv_sem,
):
    dp_count, tensor_count = place.dp_count, place.tensor_count
    links = Links(send_sem, recv_sem)
    block, features = x_ref.shape
    length = ogr_ref.shape[0]
    heads = band_ref.shape[1] // 8
    top_count = gate_rows.shape[0]
    experts = sent_ref.shape[0]
    slots_one = sent_ref.shape[1] * sent_ref.shape[2]
    own = place.own_rows(block)
    place.greet()
    for load in loads[:-2]:
        load.wait()
    rows_ref[0, own, :] = x_ref[...].astype(BF16)
    ogr_ref[own, :] = og_ref[...].astype(BF16)
    piece = gain1.shape[0]
    own_gains = jnp.concatenate(
        [gain[...].reshape(1, piece) for gain in (gain1, gain2, gain3, gain4)], axis=0
    )
    spot = place_values(piece, (place.dp * tensor_count + place.rank) * piece, features)
    gains = mm(own_gains, spot)
    biases = [
        mm(bias[...], place_values(bias.shape[0], place.dp * bias.shape[0], 128), 0, 0)
        for bias in (bias1, bias2)
    ]
    biases.append(jnp.zeros((heads, features - 256), F32))
    small_ref[...] = jnp.concatenate(
        [gains, jnp.zeros((8 - gains.shape[0], features), F32),
         jnp.concatenate(biases, axis=1), jnp.zeros((8 - heads, features), F32)], axis=0
    ).astype(BF16)
    for full_ref, blocks, last in (
        (w1f_ref, (query1, key1, value1), output1), (w2f_ref, (query2, key2, value2), output2)
    ):
        turned = last[...].astype(F32).T.astype(BF16)
        full_ref[place.dp] = jnp.concatenate([*[ref[...] for ref in blocks], turned], axis=1)
    wdf_ref[place.dp] = jnp.concatenate([dense_up[...], dense_down[...]], axis=1)
    place.met()

    small_land[place.rank] = small_ref[...]
    small_z = [
        links.push(small_ref, small_land.at[place.rank], {"tensor": place.rank_at(offset)})
        for offset in range(1, tensor_count)
    ]
    x_copies = spread_rows(links, place, rows_ref.at[0], block)
    one_started = gather_start(links, place, w1f_ref)
    for load in loads[-2:]:
        load.start()
    wait_all(small_z)
    gains = small_land[0, 0:8, :].astype(F32)
    for rank in range(1, tensor_count):
        gains = gains + small_land[rank, 0:8, :].astype(F32)
    small_full[place.dp] = jnp.concatenate(
        [gains, small_ref[8:16, :].astype(F32)], axis=0
    ).astype(BF16)
    small_dp = [
        links.push(small_full.at[place.dp], small_full.at[place.dp], {"dp": place.dp_at(offset)})
        for offset in range(1, dp_count)
    ]
    og_copies = spread_rows(links, place, ogr_ref, block)
    one_passed = gather_forward(links, place, one_started, w1f_ref)
    dense_started = gather_start(links, place, wdf_ref)
    seg_row = segr_ref[...].astype(F32)
    slots = slot_rows(routes_ref, dp_count, experts, sent_ref.shape[2])
    slot_ref[...] = jnp.concatenate(slots, axis=1).astype(jnp.int32)
    lines = [*slots, *[gate_rows[c : c + 1, :] for c in range(top_count)], seg_row]
    lines.append(jnp.zeros((8 - len(lines), length), F32))
    columns_ref[...] = jnp.concatenate(lines, axis=0).T
    allowed = allowed_pairs(seg_row, columns_ref[:, 2 * top_count : 2 * top_count + 1])
    wait_all(small_dp)
    smalls = small_full[0].astype(F32)
    for peer in range(1, dp_count):
        smalls = smalls + small_full[peer].astype(F32)
    gains_ref[...] = smalls[0:8, :]
    make_bands(smalls[8:16, :], onehot_ref, (band_ref.at[0], band_ref.at[1]), heads)
    wait_all(x_copies)
    wait_all(one_passed)

    attn_forward(rows_ref[0], gains_ref[0:1, :], flat(w1f_ref), band_ref.at[0], allowed,
                 qkv_ref.at[0], o_ref.at[0], part_ref.at[0], shares_ref.at[0])
    copies = scatter_rows(links, place, part_ref.at[0], land_ref.at[0], block)
    wait_all(og_copies)
    out_rows = ogr_ref[...].astype(F32)
    scaled = jnp.concatenate(
        [(columns_ref[:, top_count + c : top_count + c + 1] * out_rows).astype(BF16) for c in range(top_count)],
        axis=0,
    )
    for e in range(experts):
        chosen = slot_places(slots_one, slot_ref[...] - e * slots_one).astype(BF16)
        sentg_ref[e] = mm(chosen, scaled).astype(BF16).reshape(sentg_ref.shape[1:])
    total, copies = settle(
        links, place, copies, part_ref.at[0], land_ref.at[0], cut(x_ref), rows_ref.at[1]
    )
    dense_passed = gather_forward(links, place, dense_started, wdf_ref)
    two_started = gather_start(links, place, w2f_ref)
    wait_all(copies)
    wait_all(dense_passed)

    hidden = pre_ref.shape[1]
    normed, _, _ = norm_rows(rows_ref[1], gains_ref[1:2, :])
    weights = flat(wdf_ref)
    pre = mm(normed, weights[:, :hidden])
    pre_ref[...] = pre
    active_ref[...] = gelu_value(pre).astype(BF16)
    part_ref[1] = mm(active_ref[...], weights[:, hidden:], 1, 1).astype(BF16)
    copies = scatter_rows(links, place, part_ref.at[1], land_ref.at[1], block)
    two_passed = gather_forward(links, place, two_started, w2f_ref)
    pre_ref[...] = gelu_slope(pre_ref[...])
    arrg_copies = [
        swap_start(links, place, sentg_ref, arrg_ref, e) for e in range(experts)
    ]
    total, copies = settle(
        links, place, copies, part_ref.at[1], land_ref.at[1], total, rows_ref.at[2]
    )
    wait_all(copies)
    wait_all(two_passed)

    attn_forward(rows_ref[2], gains_ref[2:3, :], flat(w2f_ref), band_ref.at[1], allowed,
                 qkv_ref.at[1], o_ref.at[1], part_ref.at[2], shares_ref.at[1])
    copies = scatter_rows(links, place, part_ref.at[2], land_ref.at[2], block)
    total, copies = settle(
        links, place, copies, part_ref.at[2], land_ref.at[2], total, rows_ref.at[3]
    )
    x3_ref[...] = jnp.concatenate(total, axis=0)
    wait_all(copies)
    normed, _, _ = norm_rows(rows_ref[3], gains_ref[3:4, :])
    arr_copies = []
    for e in range(experts):
        slot_row = slot_ref[...] - e * slots_one
        chosen = slot_places(slots_one, slot_row[:, :length]) | slot_places(
            slots_one, slot_row[:, length:]
        )
        sent_ref[e] = mm(chosen.astype(BF16), normed).astype(BF16).reshape(sent_ref.shape[1:])
        arr_copies.append(swap_start(links, place, sent_ref, arr_ref, e))
    for load in loads[-2:]:
        load.wait()

    back_copies, y_copies = [], []
    for e in range(experts):
        wait_all(arrg_copies[e])
        grad_active = mm(flat(arrg_ref.at[e]), down_ref[e], 1, 1)
        wait_all(arr_copies[e])
        active, slope = gelu_both(mm(flat(arr_ref.at[e]), up_ref[e]))
        act_ref[e] = active.astype(BF16)
        gp_ref[e] = (grad_active * slope).astype(BF16)
        back_ref[e] = mm(gp_ref[e], up_ref[e], 1, 1).astype(BF16).reshape(back_ref.shape[1:])
        back_copies.append(swap_start(links, place, back_ref, backland_ref, e))
    for e in range(experts):
        y_ref[e] = mm(act_ref[e], down_ref[e]).astype(BF16).reshape(y_ref.shape[1:])
        y_copies.append(swap_start(links, place, y_ref, yland_ref, e))

    for store in stores[2:6]:
        store.start()
    lanes = lax.broadcasted_iota(jnp.int32, (length, slots_one), 1)
    normed, normal, inv_rms = norm_rows(rows_ref[3], gains_ref[3:4, :])
    grad_normed = jnp.zeros((length, features), F32)
    for e in range(experts):
        slot_cols = columns_ref[:, 0:top_count].astype(jnp.int32) - e * slots_one
        chosen = (lanes == slot_cols[:, 0:1]) | (lanes == slot_cols[:, 1:2])
        wait_all(back_copies[e])
        grad_normed = grad_normed + mm(chosen.astype(BF16), flat(backland_ref.at[e]))
    grad_part, gain_grad[3:4, :] = norm_back(grad_normed, normal, inv_rms, gains_ref[3:4, :])
    part_ref[3] = grad_part.astype(BF16)
    copies = scatter_rows(links, place, part_ref.at[3], land_ref.at[3], block)
    total, copies = settle(
        links, place, copies, part_ref.at[3], land_ref.at[3], cut(og_ref), grows_ref.at[0]
    )
    normed_rows = norm_rows(rows_ref[2], gains_ref[2:3, :])
    wait_all(copies)

    kept = attn_backward(
        grows_ref[0], normed_rows, gains_ref[2:3, :], flat(w2f_ref), shares_ref.at[1],
        qkv_ref.at[1], o_ref.at[1], part_ref.at[4], gain_grad.at[2:3, :], score_ref,
    )
    copies = scatter_rows(links, place, part_ref.at[4], land_ref.at[4], block)
    attn_weights_grad(grows_ref[0], kept, wg2_ref)
    two_sum = sum_start(links, place, wg2_ref, pair2_ref)
    band_sums(score_ref, bandg_ref.at[1])
    total, copies = settle(
        links, place, copies, part_ref.at[4], land_ref.at[4], total, grows_ref.at[1]
    )
    two_copies = sum_onward(links, place, two_sum, wg2_ref, pair2_ref, sum2_ref)
    combined = jnp.zeros((length, features), F32)
    for e in range(experts):
        wait_all(y_copies[e])
        returned = flat(yland_ref.at[e])
        slot_cols = columns_ref[:, 0:top_count].astype(jnp.int32) - e * slots_one
        for c in range(top_count):
            chosen = (lanes == slot_cols[:, c : c + 1]).astype(BF16)
            combined = combined + columns_ref[:, top_count + c : top_count + c + 1] * mm(chosen, returned)
    part_ref[5] = combined.astype(BF16)
    normed, normal, inv_rms = norm_rows(rows_ref[1], gains_ref[1:2, :])
    wait_all(copies)
    out_copies = scatter_rows(
        links, place, part_ref.at[5], land_ref.at[5], block, range(PIECES // 2)
    )

    grad_rows = grows_ref[1]
    weights = flat(wdf_ref)
    grad_pre = (mm(grad_rows, weights[:, hidden:]) * pre_ref[...]).astype(BF16)
    grad_normed = mm(grad_pre, weights[:, :hidden], 1, 1)
    grad_part, gain_grad[1:2, :] = norm_back(grad_normed, normal, inv_rms, gains_ref[1:2, :])
    part_ref[6] = grad_part.astype(BF16)
    copies = scatter_rows(links, place, part_ref.at[6], land_ref.at[6], block)
    wgd_ref[:, :, :, :hidden] = mm(normed, grad_pre, 0, 0).astype(BF16).reshape(
        *wgd_ref.shape[:3], hidden
    )
    wgd_ref[:, :, :, hidden:] = mm(grad_rows, active_ref[...], 0, 0).astype(BF16).reshape(
        *wgd_ref.shape[:3], hidden
    )
    dense_sum = sum_start(links, place, wgd_ref, paird_ref)
    total, copies = settle(
        links, place, copies, part_ref.at[6], land_ref.at[6], total, grows_ref.at[2]
    )
    dense_copies = sum_onward(links, place, dense_sum, wgd_ref, paird_ref, sumd_ref)
    bias_two = bias_sums(bandg_ref.at[1], onehot_ref, heads)
    normed_rows = norm_rows(rows_ref[0], gains_ref[0:1, :])
    wait_all(copies)
    out_copies += scatter_rows(
        links, place, part_ref.at[5], land_ref.at[5], block, range(PIECES // 2, PIECES)
    )

    kept = attn_backward(
        grows_ref[2], normed_rows, gains_ref[0:1, :], flat(w1f_ref), shares_ref.at[0],
        qkv_ref.at[0], o_ref.at[0], part_ref.at[7], gain_grad.at[0:1, :], score_ref,
    )
    gain_grad[4:8, :] = jnp.zeros((4, features), F32)
    gain_z = [
        links.push(gain_grad, gain_land.at[offset - 1], {"tensor": place.rank_at(offset)})
        for offset in range(1, tensor_count)
    ]
    copies = scatter_rows(links, place, part_ref.at[7], land_ref.at[7], block)
    attn_weights_grad(grows_ref[2], kept, wg1_ref)
    one_sum = sum_start(links, place, wg1_ref, pair1_ref)
    one_copies = sum_onward(links, place, one_sum, wg1_ref, pair1_ref, sum1_ref)
    gains = gain_grad[...]
    for offset, copy in enumerate(gain_z):
        copy.wait_recv()
        gains = gains + gain_land[offset]
    gain_full[place.dp] = gains
    last = [
        links.push(gain_full.at[place.dp], gain_full.at[place.dp], {"dp": place.dp_at(offset)})
        for offset in range(1, dp_count)
    ]
    band_sums(score_ref, bandg_ref.at[0])
    bias_grad[...] = jnp.concatenate(
        [bias_sums(bandg_ref.at[0], onehot_ref, heads), bias_two], axis=1
    )
    bias_full[place.dp] = bias_grad[...]
    last += [
        links.push(bias_grad, bias_full.at[place.dp], {"dp": place.dp_at(offset)})
        for offset in range(1, dp_count)
    ]
    sums, _ = settle(links, place, out_copies, part_ref.at[5], land_ref.at[5], cut(x3_ref))
    out_ref[...] = jnp.concatenate(sums, axis=0)
    stores[0].start()
    total, _ = settle(links, place, copies, part_ref.at[7], land_ref.at[7], total)
    xg_ref[...] = jnp.concatenate(total, axis=0)
    stores[1].start()
    wait_all(two_copies)
    stores[8].start()
    wait_all(dense_copies)
    stores[7].start()
    wait_all(one_copies)
    stores[6].start()
    wait_all(last)
    stores[9].start()
    stores[10].start()
    links.finish()


def finish_kernel(
    *refs,
):
    sources, refs = refs[:11], refs[11:]
    held, load_sem, refs = refs[-12:-1], refs[-1], refs[:-12]
    loads = [
        pltpu.make_async_copy(source, target, load_sem.at[k])
        for k, (source, target) in enumerate(zip(sources, held))
    ]
    experts = held[2].shape[0]
    parts = [
        [
            pltpu.make_async_copy(
                sources[k].at[e], held[k].at[e], load_sem.at[11 + e * 4 + k]
            )
            for k in range(4)
        ]
        for e in range(experts)
    ]
    for e in range(experts):
        parts[e][1].start()
        parts[e][2].start()
    for k in (9, 10, 4, 6, 5, 7, 8):
        loads[k].start()
    for e in range(experts):
        parts[e][0].start()
        parts[e][3].start()
    arr_ref, arrg_ref, act_ref, gp_ref, sum1_ref, sumd_ref, sum2_ref, gain_full, bias_full = held[:9]
    layer_ref, grad_ref = held[9:]
    layer_out, grad_out, *refs = refs
    gain_outs, bias_outs = refs[:4], refs[4:6]
    refs = refs[6:]
    outs, (upg_out, downg_out) = refs[:10], refs[10:12]
    stages, (upg_ref, downg_ref), sem = refs[12:22], refs[22:24], refs[24]
    copies = []

    def send(source, target):
        copy = pltpu.make_async_copy(source, target, sem.at[len(copies)])
        copy.start()
        copies.append(copy)

    for e in range(experts):
        parts[e][1].wait()
        parts[e][2].wait()
        downg_ref[e] = mm(act_ref[e], flat(arrg_ref.at[e]), 0, 0)
        send(downg_ref.at[e], downg_out.at[e])
    for k in (9, 10, 4, 6, 5, 7, 8):
        loads[k].wait()
    send(layer_ref, layer_out)
    send(grad_ref, grad_out)

    def added(ref):
        total = ref[0].astype(F32)
        for k in range(1, ref.shape[0]):
            total = total + ref[k].astype(F32)
        return total

    one, two, dense = added(sum1_ref), added(sum2_ref), added(sumd_ref)
    width, hidden = one.shape[1] // 4, dense.shape[1] // 2
    values = []
    for total in (one, two):
        values += [total[:, k * width : (k + 1) * width] for k in range(3)]
        values.append(total[:, 3 * width :].T)
    values += [dense[:, :hidden], dense[:, hidden:]]
    for value, stage, out in zip(values, stages, outs):
        stage[...] = value
        send(stage, out)
    for e in range(experts):
        parts[e][0].wait()
        parts[e][3].wait()
        upg_ref[e] = mm(flat(arr_ref.at[e]), gp_ref[e], 0, 0)
        send(upg_ref.at[e], upg_out.at[e])
    piece = gain_outs[0].shape[0]
    me = lax.axis_index("dp")
    start = (me * lax.axis_size("tensor") + lax.axis_index("tensor")) * piece
    gains = added(gain_full)
    features = gains.shape[1]
    gains = pltpu.roll(gains, lax.rem(features - start, features), 1)
    for k, out in enumerate(gain_outs):
        out[...] = gains[k, :piece]
    biases = added(bias_full)
    count, heads = bias_outs[0].shape
    for layer, out in enumerate(bias_outs):
        block = biases[:, layer * 128 : layer * 128 + 128]
        block = pltpu.roll(block, lax.rem(128 - me * count, 128), 1)
        out[...] = block.T[:count, :heads]
    for copy in copies:
        copy.wait()


def on_device(
    layer_input, segments, routes, gate_weights,
    first_gain, first_query, first_key, first_value, first_output, first_bias,
    first_dense_gain, first_dense_up, first_dense_down,
    second_gain, second_query, second_key, second_value, second_output, second_bias,
    second_expert_gain, expert_up, expert_down, output_grad,
):
    dp_count, tensor_count = lax.axis_size("dp"), lax.axis_size("tensor")
    length = segments.shape[1]
    features = layer_input.shape[1]
    width = first_query.shape[1]
    heads = first_bias.shape[1]
    hidden = first_dense_up.shape[1]
    top_count = routes.shape[1]
    local_experts = expert_up.shape[0]
    expert_count = local_experts * dp_count
    capacity = max(2, 3 * length * top_count // (2 * expert_count))
    capacity = -(-capacity // 16) * 16
    swap_shape = (local_experts, dp_count, capacity, features)
    slots_one = dp_count * capacity
    weight_rows = first_query.shape[0]
    block = layer_input.shape[0]
    wide = 4 * width
    groups = dp_count // 2
    outs = [
        ((block, features), F32), ((block, features), F32), (swap_shape, BF16), (swap_shape, BF16),
        ((local_experts, slots_one, hidden), BF16), ((local_experts, slots_one, hidden), BF16),
        ((groups, weight_rows, wide), BF16), ((groups, weight_rows, 2 * hidden), BF16),
        ((groups, weight_rows, wide), BF16),
        ((dp_count, 8, features), F32), ((dp_count, 8, 256), F32),
    ]
    full = lambda columns: pltpu.VMEM((dp_count, weight_rows, columns), BF16)
    split = lambda columns: pltpu.VMEM((groups, 2, weight_rows, columns), BF16)
    half = lambda columns: pltpu.VMEM((groups, weight_rows, columns), BF16)
    columns = (wide, 2 * hidden, wide)
    copies = 14 * PIECES * tensor_count + 12 * tensor_count + 18 * dp_count
    inputs = (
        layer_input, output_grad, segments, routes.T, gate_weights.T,
        jnp.asarray(band_steps(length, BUCKETS), BF16),
        first_gain, first_dense_gain, second_gain, second_expert_gain,
        first_query, first_key, first_value, first_output, first_bias,
        first_dense_up, first_dense_down.T,
        second_query, second_key, second_value, second_output, second_bias,
        expert_up, expert_down,
    )
    scratch = [
        *[pltpu.VMEM(shape, dtype) for shape, dtype in outs],
        pltpu.VMEM((4, length, features), BF16),
        pltpu.VMEM((3, length, features), BF16),
        pltpu.VMEM((length, features), BF16),
        pltpu.VMEM((8, length, features), BF16),
        pltpu.VMEM((8, tensor_count - 1, block, features), BF16),
        pltpu.VMEM((8, features), F32),
        pltpu.VMEM((2, heads * 8, length), F32),
        pltpu.VMEM((2, heads * 8, length), F32),
        *[full(n) for n in columns],
        pltpu.VMEM((2, length, 3 * width), BF16),
        pltpu.VMEM((2, length, width), BF16),
        pltpu.VMEM((length, hidden), F32),
        pltpu.VMEM((block, features), F32),
        pltpu.VMEM((tensor_count, 16, features), BF16),
        pltpu.VMEM((dp_count, 16, features), BF16),
        *[pltpu.VMEM(swap_shape, BF16)] * 6,
        *[split(n) for n in columns],
        *[half(n) for n in columns],
        pltpu.VMEM((8, features), F32),
        pltpu.VMEM((tensor_count - 1, 8, features), F32),
        pltpu.VMEM((8, 256), F32),
        pltpu.VMEM((16, features), BF16),
        pltpu.VMEM((1, top_count * length), jnp.int32),
        pltpu.VMEM((length, 8), F32),
        pltpu.VMEM((2, heads, length, length), F32),
        pltpu.VMEM((heads, length, length), F32),
        pltpu.VMEM((length, hidden), BF16),
        pltpu.SemaphoreType.DMA((copies,)),
        pltpu.SemaphoreType.DMA((copies,)),
        *[pltpu.VMEM(one.shape, one.dtype) for one in inputs],
        pltpu.SemaphoreType.DMA((len(inputs) + len(outs),)),
    ]
    vmem = pl.BlockSpec(memory_space=pltpu.VMEM)
    anywhere = pl.BlockSpec(memory_space=pl.ANY)
    made = pl.pallas_call(
        functools.partial(chain_kernel, dp_count, tensor_count),
        out_shape=[jax.ShapeDtypeStruct(shape, dtype) for shape, dtype in outs],
        in_specs=[anywhere] * len(inputs),
        out_specs=[anywhere] * len(outs),
        scratch_shapes=scratch,
        compiler_params=pltpu.CompilerParams(
            collective_id=1, has_side_effects=True, vmem_limit_bytes=60 * 1024 * 1024
        ),
    )(*inputs)
    layer_sum, grad_sum, *kept = made
    four = [(weight_rows, width)] * 3 + [(width, weight_rows)]
    pieces = four + four + [(weight_rows, hidden), (weight_rows, hidden)]
    shapes = [(block, features), (block, features), *[first_gain.shape] * 4,
              *[first_bias.shape] * 2, *pieces, expert_up.shape, expert_down.shape]
    finished = pl.pallas_call(
        finish_kernel,
        out_shape=[jax.ShapeDtypeStruct(shape, F32) for shape in shapes],
        in_specs=[anywhere] * 11,
        out_specs=[anywhere] * 2 + [vmem] * 6 + [anywhere] * 12,
        scratch_shapes=[
            *[pltpu.VMEM(shape, F32) for shape in pieces],
            pltpu.VMEM(expert_up.shape, F32),
            pltpu.VMEM(expert_down.shape, F32),
            pltpu.SemaphoreType.DMA((12 + 2 * local_experts,)),
            *[pltpu.VMEM(shape, dtype) for shape, dtype in outs[2:] + outs[:2]],
            pltpu.SemaphoreType.DMA((11 + 4 * local_experts,)),
        ],
        compiler_params=pltpu.CompilerParams(vmem_limit_bytes=60 * 1024 * 1024),
    )(*kept, layer_sum, grad_sum)
    layer_output, input_grad, *grads = finished
    gains, biases, grads = grads[:4], grads[4:6], grads[6:]
    return (
        layer_output, input_grad,
        gains[0], *grads[0:4], biases[0],
        gains[1], grads[8], grads[9].T,
        gains[2], *grads[4:8], biases[1],
        gains[3], *grads[10:],
    )


def solution(mesh):
    attn = (P("dp", "tensor"), P("dp", "tensor"), P("dp", "tensor"), P("tensor", "dp"),
            P("dp", "tensor"))
    both = P(("dp", "tensor"))
    rows = P(("dp", "tensor"), None)
    return jax.shard_map(
        on_device,
        mesh=mesh,
        in_specs=(
            rows, P("dp", None), P("dp", None), P("dp", None),
            both, *attn,
            both, P("dp", "tensor"), P("tensor", "dp"),
            both, *attn,
            both, P("dp", None, "tensor"), P("dp", "tensor", None), rows,
        ),
        out_specs=(
            rows, rows,
            both, *attn,
            both, P("dp", "tensor"), P("tensor", "dp"),
            both, *attn,
            both, P("dp", None, "tensor"), P("dp", "tensor", None),
        ),
        check_vma=False,
    )
```
